32 devices in a mesh: groups: 2 (over x), seq: 4 (over y, core), head: 4 (over z).
Axes of the slice: x: 2, y: 2, z: 4, core: 2. Of those that a mesh axis runs over, the one named last changes fastest.
Arguments:
- patches: bfloat16 [32768, 1024], P(('groups', 'seq')), parts along dimension 0, may hold values from -100 to 100, as said below
- w_qkv: bfloat16 [1024, 3, 1024], P(None, None, 'head'), may hold values from -0.1875 to 0.1875
Outputs:
- mixed: bfloat16 [32768, 1024], P(('groups', 'seq'), 'head'), parts along dimension 0
The draws below stay inside these ranges and needn't reach their ends.
There are 2 independent parts, one for each index of `groups`. The reference program is written for one: setup_inputs(seed, part) draws one part's arguments, and reference() takes and returns one part's arrays. A program takes and returns all parts, laid end to end along the dimension named above; an argument that names none is the same for every part. Nothing has to cross between parts.
Inputs may be any that keep to these rules, and one draw needn't show every extreme that they name: `patches`: entries are finite.
All inputs are finite; a program needn't handle non-finite values.
Results may differ from the reference program's by a relative error of at most 0.0012.
The reference program's roundings to bfloat16 on the way count: a program that leaves them out, or rounds other values in their place, can miss the bound.
Values may be sent and summed in bfloat16 or wider, within the bound.
No kernel may reach another device: no remote copies, remote signals or barrier semaphores. Data moves between devices by JAX's collectives and lax.ppermute only.
A program may use at most 192 MiB of HBM per device.

```python
import math
import jax
import jax.numpy as jnp
from jax import lax

D = 1024
HEADS = 16
HEAD_DIM = 64
COLS = 256
ROWS = 64
TOKENS = 16384


def draw_patches(key, part):
    keys_all = jax.random.split(jax.random.fold_in(key, 11), 1)
    base = jax.random.normal(keys_all[0], (TOKENS, D), jnp.float32)
    return jnp.clip(base, -6.0, 6.0).astype(jnp.bfloat16)


def levels(own_key, shape, cuts, low, high):
    loudness, own = 1.0, jax.random.fold_in(own_key, 6)
    for axis_at, parts in cuts:
        steps = jnp.exp(jax.random.uniform(jax.random.fold_in(own, axis_at), (parts,), jnp.float32, low / len(cuts), high / len(cuts)))
        loudness = loudness * jnp.repeat(steps, shape[axis_at] // parts).reshape([-1 if axis == axis_at else 1 for axis in range(len(shape))])
    return loudness


def bell_draw(own_key, dims, deviation, reach, shards=(), dtype=jnp.bfloat16):
    values = jax.random.normal(own_key, dims, jnp.float32) * deviation
    if len(shards) > 0:
        values = levels(own_key, dims, shards, -0.22, 0.18) * values
    return jnp.clip(values, min=-reach, max=reach).astype(dtype)


def setup_inputs(seed: int = 0, part: int = 0) -> dict:
    arg_keys = jax.random.split(jax.random.key(seed), 3)
    part_keys = jax.random.split(jax.random.fold_in(arg_keys[2], part), 3)
    return {
        "patches": draw_patches(jax.random.fold_in(jax.random.fold_in(arg_keys[2], part), 71), part),
        "w_qkv": bell_draw(arg_keys[1], (D, 3, D), D ** -0.5, 0.1875, ((2, 4),)),
    }


NEG_BIG = -1e+30

def row_attention(queries, key_rows, value_rows):
    row_count = queries.shape[0]
    prev_keys = jnp.zeros_like(key_rows[0])
    prev_values = jnp.zeros_like(value_rows[0])
    earlier_keys = jnp.concatenate([prev_keys[None], key_rows[:-1]], 0)
    earlier_values = jnp.concatenate([prev_values[None], value_rows[:-1]], 0)
    joined_keys = jnp.concatenate([earlier_keys, key_rows], 1)
    joined_values = jnp.concatenate([earlier_values, value_rows], 1)
    scores = jnp.einsum('rcd,rjd->rcj', queries.astype(jnp.float32), joined_keys.astype(jnp.float32)) * (1.0 / math.sqrt(HEAD_DIM))
    column = lax.broadcasted_iota(jnp.int32, (1, COLS, 2 * COLS), 1)
    slot = lax.broadcasted_iota(jnp.int32, (1, COLS, 2 * COLS), 2)
    row_index = lax.broadcasted_iota(jnp.int32, (row_count, 1, 1), 0)
    allowed = (slot > column) & (slot <= column + COLS) & ((slot >= COLS) | (row_index > 0))
    scores = jnp.where(allowed, scores, NEG_BIG)
    highest = lax.optimization_barrier(jnp.max(scores, axis=-1, keepdims=True))
    terms = jnp.where(allowed, jnp.exp(scores - highest), 0.0)
    totals = lax.optimization_barrier(jnp.sum(terms, axis=-1, keepdims=True))
    rounded = terms.astype(jnp.bfloat16)
    context = jnp.einsum('rcj,rjd->rcd', rounded.astype(jnp.float32), joined_values.astype(jnp.float32))
    return context / totals

def column_attention(queries, key_rows, value_rows):
    row_count = queries.shape[0]
    scores = jnp.einsum('rcd,scd->crs', queries.astype(jnp.float32), key_rows.astype(jnp.float32)) * (1.0 / math.sqrt(HEAD_DIM))
    later = lax.broadcasted_iota(jnp.int32, (1, row_count, row_count), 1)
    earlier = lax.broadcasted_iota(jnp.int32, (1, row_count, row_count), 2)
    allowed = earlier <= later
    scores = jnp.where(allowed, scores, NEG_BIG)
    highest = lax.optimization_barrier(jnp.max(scores, axis=-1, keepdims=True))
    terms = jnp.where(allowed, jnp.exp(scores - highest), 0.0)
    totals = lax.optimization_barrier(jnp.sum(terms, axis=-1, keepdims=True))
    rounded = terms.astype(jnp.bfloat16)
    context = jnp.einsum('crs,scd->rcd', rounded.astype(jnp.float32), value_rows.astype(jnp.float32))
    return (context / jnp.transpose(totals, (1, 0, 2))).astype(jnp.bfloat16)

def one_head(pack):
    queries, key_rows, value_rows = pack
    row_part = row_attention(queries, key_rows, value_rows)
    column_part = column_attention(queries, key_rows, value_rows)
    return (0.5 * (row_part + column_part.astype(jnp.float32))).astype(jnp.bfloat16)

def split_heads(flat):
    return jnp.transpose(flat.reshape(ROWS, COLS, HEADS, HEAD_DIM), (2, 0, 1, 3))

def reference(patches, w_qkv):
    queries = jnp.dot(patches, w_qkv[:, 0, :], preferred_element_type=jnp.float32).astype(jnp.bfloat16)
    key_rows = jnp.dot(patches, w_qkv[:, 1, :], preferred_element_type=jnp.float32).astype(jnp.bfloat16)
    value_rows = jnp.dot(patches, w_qkv[:, 2, :], preferred_element_type=jnp.float32).astype(jnp.bfloat16)
    result = lax.map(one_head, (split_heads(queries), split_heads(key_rows), split_heads(value_rows)))
    return jnp.transpose(result, (1, 2, 0, 3)).reshape(TOKENS, D)
```

```python
import functools
import math

import jax
import jax.numpy as jnp
from jax import lax
from jax.experimental import pallas as pl
from jax.experimental.pallas import tpu as pltpu
from jax.sharding import PartitionSpec as P

D = 1024
HEAD_DIM = 64
COLS = 256
NEG_BIG = -1e30

STRIP = 16
BOTH = 2 * STRIP
TILE = 16
PACK = 4

F32 = jnp.float32
BF16 = jnp.bfloat16


def shifted(block, axis, distance):
    devices = range(lax.axis_size(axis))
    route = [(i - distance, i) for i in devices if i - distance in devices]
    return lax.ppermute(block, axis, route)


def row_attention(queries, key_rows, value_rows, prev_keys, prev_values, first_row):
    row_count = queries.shape[1]
    scale = 1.0 / math.sqrt(HEAD_DIM)
    earlier_keys = jnp.concatenate([prev_keys[:, None], key_rows[:, :-1]], 1)
    earlier_values = jnp.concatenate([prev_values[:, None], value_rows[:, :-1]], 1)
    score_prev = (
        jnp.einsum("hrce,hrje->hrcj", queries, earlier_keys, preferred_element_type=jnp.float32)
        * scale
    )
    score_own = (
        jnp.einsum("hrce,hrje->hrcj", queries, key_rows, preferred_element_type=jnp.float32) * scale
    )
    column = lax.broadcasted_iota(jnp.int32, (1, 1, COLS, COLS), 2)
    slot = lax.broadcasted_iota(jnp.int32, (1, 1, COLS, COLS), 3)
    row_index = lax.broadcasted_iota(jnp.int32, (1, row_count, 1, 1), 1) + first_row
    allowed_prev = (slot > column) & (row_index > 0)
    allowed_own = slot <= column
    score_prev = jnp.where(allowed_prev, score_prev, NEG_BIG)
    score_own = jnp.where(allowed_own, score_own, NEG_BIG)
    highest = jnp.maximum(
        jnp.max(score_prev, axis=-1, keepdims=True), jnp.max(score_own, axis=-1, keepdims=True)
    )
    terms_prev = jnp.where(allowed_prev, jnp.exp(score_prev - highest), 0.0)
    terms_own = jnp.where(allowed_own, jnp.exp(score_own - highest), 0.0)
    totals = jnp.sum(terms_prev, axis=-1, keepdims=True) + jnp.sum(
        terms_own, axis=-1, keepdims=True
    )
    context = jnp.einsum(
        "hrcj,hrje->hrce",
        terms_prev.astype(jnp.bfloat16),
        earlier_values,
        preferred_element_type=jnp.float32,
    )
    context = context + jnp.einsum(
        "hrcj,hrje->hrce",
        terms_own.astype(jnp.bfloat16),
        value_rows,
        preferred_element_type=jnp.float32,
    )
    return context / totals


def column_attention(queries, key_rows, value_rows):
    row_count = queries.shape[1]
    scores = jnp.einsum(
        "hrce,hsce->hcrs", queries, key_rows, preferred_element_type=jnp.float32
    ) * (1.0 / math.sqrt(HEAD_DIM))
    later = lax.broadcasted_iota(jnp.int32, (1, 1, row_count, row_count), 2)
    earlier = lax.broadcasted_iota(jnp.int32, (1, 1, row_count, row_count), 3)
    allowed = earlier <= later
    scores = jnp.where(allowed, scores, NEG_BIG)
    highest = jnp.max(scores, axis=-1, keepdims=True)
    terms = jnp.where(allowed, jnp.exp(scores - highest), 0.0)
    totals = jnp.sum(terms, axis=-1, keepdims=True)
    context = jnp.einsum(
        "hcrs,hsce->hcre",
        terms.astype(jnp.bfloat16),
        value_rows,
        preferred_element_type=jnp.float32,
    )
    return jnp.transpose((context / totals).astype(jnp.bfloat16), (0, 2, 1, 3))


def general(patches, w_qkv):
    local_width = w_qkv.shape[2]
    head_count = local_width // HEAD_DIM
    row_count = patches.shape[0] // COLS
    weights_heads = w_qkv.reshape(D, 3, head_count, HEAD_DIM)
    projected = jnp.einsum(
        "td,dkhe->khte", patches, weights_heads, preferred_element_type=jnp.float32
    ).astype(jnp.bfloat16)
    prev_inputs = shifted(patches[-COLS:], "seq", 1)
    prev_pair = jnp.einsum(
        "td,dkhe->khte", prev_inputs, weights_heads[:, 1:], preferred_element_type=jnp.float32
    ).astype(jnp.bfloat16)
    first_row = lax.axis_index("seq") * row_count
    stacked = projected.reshape(3, head_count, row_count, COLS, HEAD_DIM)
    row_context = row_attention(
        stacked[0], stacked[1], stacked[2], prev_pair[0], prev_pair[1], first_row
    )
    column_pack = lax.all_to_all(stacked, "seq", split_axis=3, concat_axis=2, tiled=True)
    column_context = column_attention(column_pack[0], column_pack[1], column_pack[2])
    returned = lax.all_to_all(column_context, "seq", split_axis=1, concat_axis=2, tiled=True)
    mixed = (0.5 * (row_context + returned.astype(jnp.float32))).astype(jnp.bfloat16)
    return jnp.transpose(mixed, (1, 2, 0, 3)).reshape(row_count * COLS, local_width)


def iota(shape, axis):
    return lax.broadcasted_iota(jnp.int32, shape, axis)


def dot(left, right):
    return jnp.dot(left, right, preferred_element_type=F32)


def dot_t(left, right):
    return lax.dot_general(left, right, (((1,), (1,)), ((), ())), preferred_element_type=F32)


def cost(microseconds):
    return pl.CostEstimate(
        flops=int(microseconds * 1e9), bytes_accessed=int(microseconds * 3e6), transcendentals=0
    )


def swap_matrix():
    to = iota((TILE * STRIP, TILE * STRIP), 0)
    source = iota((TILE * STRIP, TILE * STRIP), 1)
    hit = ((to & (STRIP - 1)) << 4) + (to >> 4) == source
    return jnp.where(hit, 1.0, 0.0).astype(BF16)


def project_kernel(info, x_ref, w_ref, *refs, block, width, half_steps):
    q_ref, k_ref, v_ref, mine_ref, other_ref, send_mine_ref, send_other_ref = refs[-7:]
    step = pl.program_id(0)
    upper = info[1] == 0
    swap = swap_matrix()
    x = x_ref[...].reshape(STRIP * block, D)
    natural = []
    for i, ref in enumerate((q_ref, k_ref, v_ref)):
        value = dot(x, w_ref[i]).astype(BF16).reshape(STRIP, block, width)
        ref[...] = value
        natural.append(value)

    def store(triple_ref, send_ref):
        for g in range(block // TILE):
            part = slice(g * TILE, (g + 1) * TILE)
            pieces = []
            for i in range(3):
                tokens = natural[i][:, part, :].reshape(STRIP * TILE, width)
                piece = dot(swap, tokens).astype(BF16).reshape(TILE, STRIP, width)
                triple_ref[i, part] = piece
                pieces.append(piece)

            @pl.when(upper)
            def _():
                send_ref[part] = pieces[2]

            @pl.when(jnp.logical_not(upper))
            def _():
                send_ref[part] = pieces[0]

    @pl.when(step < half_steps)
    def _():
        store(mine_ref, send_mine_ref)

    @pl.when(step >= half_steps)
    def _():
        store(other_ref, send_other_ref)


def project(info, x, w, natural, chunk, chunk_cols, block):
    width = w.shape[2]
    half_steps = chunk_cols // block
    per_half = COLS // 2 // block
    first = chunk * half_steps

    def column_block(j, info):
        half = jnp.where(j < half_steps, info[0], 1 - info[0])
        return half * per_half + first + lax.rem(j, half_steps)

    def natural_map(j, info):
        return (0, column_block(j, info), 0)

    def mine_at(j):
        return jnp.minimum(j, half_steps - 1)

    def other_at(j):
        return jnp.maximum(j - half_steps, 0)

    natural_spec = pl.BlockSpec((STRIP, block, width), natural_map)
    out_specs = [natural_spec] * 3 + [
        pl.BlockSpec((3, block, STRIP, width), lambda j, info: (0, mine_at(j), 0, 0)),
        pl.BlockSpec((3, block, STRIP, width), lambda j, info: (0, other_at(j), 0, 0)),
        pl.BlockSpec((block, STRIP, width), lambda j, info: (mine_at(j), 0, 0)),
        pl.BlockSpec((block, STRIP, width), lambda j, info: (other_at(j), 0, 0)),
    ]
    natural_shape = jax.ShapeDtypeStruct((STRIP, COLS, width), BF16)
    triple = jax.ShapeDtypeStruct((3, chunk_cols, STRIP, width), BF16)
    single = jax.ShapeDtypeStruct((chunk_cols, STRIP, width), BF16)
    operands = [x, w]
    in_specs = [
        pl.BlockSpec((STRIP, block, D), natural_map),
        pl.BlockSpec(w.shape, lambda j, info: (0, 0, 0), pipeline_mode=pl.Buffered(1)),
    ]
    aliases = {}
    if natural is not None:
        aliases = {3: 0, 4: 1, 5: 2}
        operands += list(natural)
        in_specs += [pl.BlockSpec(memory_space=pl.ANY)] * 3
    return pl.pallas_call(
        functools.partial(project_kernel, block=block, width=width, half_steps=half_steps),
        out_shape=[natural_shape] * 3 + [triple, triple, single, single],
        grid_spec=pltpu.PrefetchScalarGridSpec(
            num_scalar_prefetch=1,
            grid=(2 * half_steps,),
            in_specs=in_specs,
            out_specs=out_specs,
        ),
        input_output_aliases=aliases,
        cost_estimate=cost(8),
        name="project",
    )(info, *operands)


def heads_of(shape, axis):
    return iota(shape, axis) // HEAD_DIM


def head_rows(rows_per_head, width):
    shape = (rows_per_head * (width // HEAD_DIM), width)
    own = iota(shape, 0) // rows_per_head == iota(shape, 1) // HEAD_DIM
    return jnp.where(own, 1.0 / math.sqrt(HEAD_DIM), 0.0).astype(BF16)


def row_kernel(info, halo_ref, w_ref, q_ref, k_ref, v_ref, out_ref, prev_k, prev_v, *, width):
    row = pl.program_id(0)
    heads = width // HEAD_DIM

    @pl.when(row == 0)
    def _():
        prev_k[...] = dot(halo_ref[...], w_ref[1]).astype(BF16)
        prev_v[...] = dot(halo_ref[...], w_ref[2]).astype(BF16)

    first = (row == 0) & (info[2] == 0)
    shut = jnp.where(first, NEG_BIG, 0.0)
    own = iota((COLS, COLS), 1) <= iota((COLS, COLS), 0)
    q = jnp.concatenate([q_ref[0]] * heads, 0) * head_rows(COLS, width)
    k = k_ref[0]
    v = v_ref[0]
    scores_own = dot_t(q, k)
    scores_prev = dot_t(q, prev_k[...])
    weights_own, weights_prev, inverses = [], [], []
    for h in range(heads):
        part = slice(h * COLS, (h + 1) * COLS)
        scores = jnp.where(own, scores_own[part], scores_prev[part] + shut)
        terms = jnp.exp(scores - jnp.max(scores, axis=1, keepdims=True))
        inverses.append(1.0 / jnp.sum(terms, axis=1, keepdims=True))
        weights_own.append(jnp.where(own, terms, 0.0).astype(BF16))
        weights_prev.append(jnp.where(own, 0.0, terms).astype(BF16))
    context = dot(jnp.concatenate(weights_own, 0), v)
    context = context + dot(jnp.concatenate(weights_prev, 0), prev_v[...])
    lane_head = heads_of((COLS, width), 1)
    result = context[:COLS] * inverses[0]
    for h in range(1, heads):
        part = slice(h * COLS, (h + 1) * COLS)
        result = jnp.where(lane_head == h, context[part] * inverses[h], result)
    out_ref[0] = result
    prev_k[...] = k
    prev_v[...] = v


def row_part(info, halo, w, q, k, v):
    width = w.shape[2]
    spec = pl.BlockSpec((1, COLS, width), lambda r, info: (r, 0, 0))
    return pl.pallas_call(
        functools.partial(row_kernel, width=width),
        out_shape=jax.ShapeDtypeStruct((STRIP, COLS, width), F32),
        grid_spec=pltpu.PrefetchScalarGridSpec(
            num_scalar_prefetch=1,
            grid=(STRIP,),
            in_specs=[
                pl.BlockSpec(halo.shape, lambda r, info: (0, 0), pipeline_mode=pl.Buffered(1)),
                pl.BlockSpec(w.shape, lambda r, info: (0, 0, 0), pipeline_mode=pl.Buffered(1)),
                spec,
                spec,
                spec,
            ],
            out_specs=spec,
            scratch_shapes=[pltpu.VMEM((COLS, width), BF16)] * 2,
        ),
        cost_estimate=cost(18),
        name="row_attention",
    )(info, halo, w, q, k, v)


def column_of(mine, other, j):
    return jnp.concatenate([mine[j], other[j]], 0)


def scores_of(keys, queries, spread, heads):
    return dot_t(keys, jnp.concatenate([queries] * heads, 0) * spread)


def later_key(core, heads):
    shape = (BOTH, heads * BOTH)
    key_row = (iota(shape, 0) + STRIP * core) & (BOTH - 1)
    query_row = (iota(shape, 1) + STRIP * core) & (BOTH - 1)
    return key_row > query_row


def maxima_kernel(info, mine_ref, other_ref, out_ref, *, heads, block):
    hidden = later_key(info[0], heads)
    spread = head_rows(BOTH, heads * HEAD_DIM)

    def body(g, carry):
        at = g * PACK
        part = pl.ds(at, PACK)
        qm, qo = mine_ref[0, part], other_ref[0, part]
        km, ko = mine_ref[1, part], other_ref[1, part]
        tops = []
        for j in range(PACK):
            scores = scores_of(column_of(km, ko, j), column_of(qm, qo, j), spread, heads)
            tops.append(jnp.max(jnp.where(hidden, NEG_BIG, scores), axis=0, keepdims=True))
        out_ref[part] = jnp.concatenate(tops, 0)
        return carry

    lax.fori_loop(0, block // PACK, body, 0)


def maxima(info, mine, other, block):
    _, cols, _, width = mine.shape
    heads = width // HEAD_DIM
    spec = pl.BlockSpec((2, block, STRIP, width), lambda j, info: (0, j, 0, 0))
    return pl.pallas_call(
        functools.partial(maxima_kernel, heads=heads, block=block),
        out_shape=jax.ShapeDtypeStruct((cols, heads * BOTH), F32),
        grid_spec=pltpu.PrefetchScalarGridSpec(
            num_scalar_prefetch=1,
            grid=(cols // block,),
            in_specs=[spec, spec],
            out_specs=pl.BlockSpec((block, heads * BOTH), lambda j, info: (j, 0)),
        ),
        cost_estimate=cost(3),
        name="maxima",
    )(info, mine, other)


def weights_kernel(info, qm_ref, qo_ref, km_ref, ko_ref, top_ref, w_ref, stats_ref, *, heads, block):
    spread = head_rows(BOTH, heads * HEAD_DIM)

    def body(g, carry):
        part = pl.ds(g * PACK, PACK)
        qm, qo = qm_ref[part], qo_ref[part]
        km, ko = km_ref[0, part], ko_ref[0, part]
        below = top_ref[part]
        tops, totals, turned = [], [], []
        for j in range(PACK):
            scores = scores_of(column_of(km, ko, j), column_of(qm, qo, j), spread, heads)
            top = jnp.maximum(jnp.max(scores, axis=0, keepdims=True), below[j : j + 1])
            terms = jnp.exp(scores - top)
            tops.append(top)
            totals.append(jnp.sum(terms, axis=0, keepdims=True))
            turned.append(terms)
        w_ref[g] = jnp.concatenate(turned, 0).T.astype(BF16)
        stats_ref[0, part] = jnp.concatenate(tops, 0)
        stats_ref[1, part] = jnp.concatenate(totals, 0)
        return carry

    @pl.when(info[1] == 0)
    def _():
        lax.fori_loop(0, block // PACK, body, 0)


def cross_weights(info, recv_mine, recv_other, mine, other, top, block):
    _, cols, _, width = mine.shape
    heads = width // HEAD_DIM
    rows = heads * BOTH
    q_spec = pl.BlockSpec((block, STRIP, width), lambda j, info: (j, 0, 0))
    k_spec = pl.BlockSpec((1, block, STRIP, width), lambda j, info: (1, j, 0, 0))
    return pl.pallas_call(
        functools.partial(weights_kernel, heads=heads, block=block),
        out_shape=[
            jax.ShapeDtypeStruct((cols // PACK, rows, PACK * BOTH), BF16),
            jax.ShapeDtypeStruct((2, cols, rows), F32),
        ],
        grid_spec=pltpu.PrefetchScalarGridSpec(
            num_scalar_prefetch=1,
            grid=(cols // block,),
            in_specs=[
                q_spec,
                q_spec,
                k_spec,
                k_spec,
                pl.BlockSpec((block, rows), lambda j, info: (j, 0)),
            ],
            out_specs=[
                pl.BlockSpec((block // PACK, rows, PACK * BOTH), lambda j, info: (j, 0, 0)),
                pl.BlockSpec((2, block, rows), lambda j, info: (0, j, 0)),
            ],
        ),
        cost_estimate=cost(4),
        name="cross_weights",
    )(info, recv_mine, recv_other, mine, other, top)


def column_kernel(
    info, mine_ref, other_ref, vm_ref, vo_ref, w_ref, stats_ref, om_ref, oo_ref, *, heads, block
):
    hidden = later_key(info[0], heads)
    width = heads * HEAD_DIM
    rows = heads * BOTH
    spread = head_rows(BOTH, width)
    lower = info[1] == 1
    pair = 2 * BOTH
    keys = PACK * BOTH
    key_column = (iota((1, 2 * keys), 1) & (keys - 1)) // BOTH
    picks = [jnp.where(key_column == j, 1.0, 0.0).astype(BF16) for j in range(PACK)]
    left_head = iota((BOTH, 2 * HEAD_DIM), 1) < HEAD_DIM

    def body(g, carry):
        part = pl.ds(g * PACK, PACK)
        qm, qo = mine_ref[0, part], other_ref[0, part]
        km, ko = mine_ref[1, part], other_ref[1, part]
        above, far_totals = stats_ref[0, part], stats_ref[1, part]
        totals, turned = [], []
        for j in range(PACK):
            scores = scores_of(column_of(km, ko, j), column_of(qm, qo, j), spread, heads)
            scores = jnp.where(hidden, NEG_BIG, scores)
            top = jnp.max(scores, axis=0, keepdims=True)
            top = jnp.where(lower, above[j : j + 1], top)
            terms = jnp.exp(scores - top)
            totals.append(jnp.sum(terms, axis=0, keepdims=True))
            turned.append(terms)
        inverse = 1.0 / (jnp.concatenate(totals, 0) + far_totals)
        inverse = jnp.concatenate([inverse, inverse], 0).T
        near = jnp.concatenate(turned, 0).T.astype(BF16)
        weights = jnp.concatenate([near, w_ref[g]], 1)
        near_v = [column_of(mine_ref[2, part], other_ref[2, part], j) for j in range(PACK)]
        far_v = [column_of(vm_ref[part], vo_ref[part], j) for j in range(PACK)]
        values = jnp.concatenate(near_v + far_v, 0)
        for t in range(heads // 2):
            lanes = slice(t * 2 * HEAD_DIM, (t + 1) * 2 * HEAD_DIM)
            half = weights[t * pair : (t + 1) * pair]
            left = jnp.concatenate([half * picks[j] for j in range(PACK)], 0)
            context = dot(left, values[:, lanes])
            for j in range(PACK):
                at = j * pair
                first = t * pair
                out = jnp.where(
                    left_head, context[at : at + BOTH], context[at + BOTH : at + 2 * BOTH]
                )
                factor = jnp.where(
                    left_head,
                    inverse[first : first + BOTH, j : j + 1],
                    inverse[first + BOTH : first + 2 * BOTH, j : j + 1],
                )
                out = (out * factor).astype(BF16)
                om_ref[g * PACK + j, :, lanes] = out[:STRIP]
                oo_ref[g * PACK + j, :, lanes] = out[STRIP:]
        return carry

    lax.fori_loop(0, block // PACK, body, 0)


def column_part(info, mine, other, recv_mine, recv_other, weights, stats, block):
    _, cols, _, width = mine.shape
    heads = width // HEAD_DIM
    rows = heads * BOTH
    triple = pl.BlockSpec((3, block, STRIP, width), lambda j, info: (0, j, 0, 0))
    single = pl.BlockSpec((block, STRIP, width), lambda j, info: (j, 0, 0))
    shape = jax.ShapeDtypeStruct((cols, STRIP, width), BF16)
    return pl.pallas_call(
        functools.partial(column_kernel, heads=heads, block=block),
        out_shape=[shape, shape],
        grid_spec=pltpu.PrefetchScalarGridSpec(
            num_scalar_prefetch=1,
            grid=(cols // block,),
            in_specs=[
                triple,
                triple,
                single,
                single,
                pl.BlockSpec((block // PACK, rows, PACK * BOTH), lambda j, info: (j, 0, 0)),
                pl.BlockSpec((2, block, rows), lambda j, info: (0, j, 0)),
            ],
            out_specs=[single, single],
        ),
        cost_estimate=cost(6),
        name="column_attention",
    )(info, mine, other, recv_mine, recv_other, weights, stats)


def mix_kernel(info, row_ref, mine_ref, other_ref, *refs, block, half_steps, width):
    out_ref = refs[-1]
    step = pl.program_id(0)
    swap = swap_matrix()

    def write(ref):
        for g in range(block // TILE):
            part = slice(g * TILE, (g + 1) * TILE)
            column = dot(swap, ref[part].reshape(TILE * STRIP, width))
            column = column.reshape(STRIP, TILE, width)
            out_ref[:, part, :] = (0.5 * (row_ref[:, part, :] + column)).astype(BF16)

    @pl.when(step < half_steps)
    def _():
        write(mine_ref)

    @pl.when(step >= half_steps)
    def _():
        write(other_ref)


def mix(info, row_context, mine, other, done, chunk, block):
    cols, _, width = mine.shape
    half_steps = cols // block
    per_half = COLS // 2 // block
    first = chunk * half_steps

    def natural_map(j, info):
        half = jnp.where(j < half_steps, info[0], 1 - info[0])
        return (0, half * per_half + first + lax.rem(j, half_steps), 0)

    in_specs = [
        pl.BlockSpec((STRIP, block, width), natural_map),
        pl.BlockSpec(
            (block, STRIP, width), lambda j, info: (jnp.minimum(j, half_steps - 1), 0, 0)
        ),
        pl.BlockSpec(
            (block, STRIP, width), lambda j, info: (jnp.maximum(j - half_steps, 0), 0, 0)
        ),
    ]
    operands = [row_context, mine, other]
    aliases = {}
    if done is not None:
        operands.append(done)
        in_specs.append(pl.BlockSpec(memory_space=pl.ANY))
        aliases = {4: 0}
    return pl.pallas_call(
        functools.partial(mix_kernel, block=block, half_steps=half_steps, width=width),
        out_shape=jax.ShapeDtypeStruct((STRIP, COLS, width), BF16),
        grid_spec=pltpu.PrefetchScalarGridSpec(
            num_scalar_prefetch=1,
            grid=(2 * half_steps,),
            in_specs=in_specs,
            out_specs=pl.BlockSpec((STRIP, block, width), natural_map),
        ),
        input_output_aliases=aliases,
        cost_estimate=cost(3),
        name="mix",
    )(info, *operands)


CORE_SWAP = [(0, 1), (1, 0), (2, 3), (3, 2)]
SAME_CORE = [(0, 2), (1, 3), (2, 0), (3, 1)]
OTHER_CORE = [(0, 3), (1, 2), (2, 1), (3, 0)]
DOWN_SAME = [(0, 2), (1, 3)]
UP_SAME = [(2, 0), (3, 1)]


def send(block, route):
    return pltpu.with_memory_space_constraint(lax.ppermute(block, "seq", route), pltpu.HBM)


def after(value, *earlier):
    return lax.optimization_barrier((value,) + earlier)[0]


def two_chips(patches, w_qkv):
    width = w_qkv.shape[2]
    chunks = 2
    chunk_cols = COLS // 2 // chunks
    block = 32
    place_on_seq = lax.axis_index("seq")
    info = jnp.stack([place_on_seq % 2, place_on_seq // 2, place_on_seq]).astype(jnp.int32)
    halo = send(patches[-COLS:], [(0, 1), (1, 2), (2, 3)])
    x = patches.reshape(STRIP, COLS, D)
    w = jnp.transpose(w_qkv, (1, 0, 2))

    natural = None
    mine, other, sends = [], [], []
    for c in range(chunks):
        outs = project(info, x, w, natural, c, chunk_cols, block)
        natural = outs[:3]
        mine.append(outs[3])
        sends.append((outs[5], outs[6]))
        other.append(send(outs[4], CORE_SWAP))
    received = []
    tops = []
    for c in range(chunks):
        received.append((send(sends[c][0], SAME_CORE), send(sends[c][1], OTHER_CORE)))
        top = maxima(info, mine[c], other[c], block)
        tops.append(send(top, UP_SAME))
    row_context = row_part(info, halo, w, *natural)
    out = None
    for c in range(chunks):
        weights, stats = cross_weights(
            info, received[c][0], received[c][1], mine[c], other[c], tops[c], block
        )
        weights = send(weights, DOWN_SAME)
        stats = send(stats, DOWN_SAME)
        near, far = column_part(
            info, mine[c], other[c], received[c][0], received[c][1], weights, stats, block
        )
        far = send(far, CORE_SWAP)
        out = mix(info, row_context, near, far, out, c, block)
    return out.reshape(STRIP * COLS, width)


def local(patches, w_qkv):
    shape_fits = patches.shape[0] == STRIP * COLS and w_qkv.shape[2] == 4 * HEAD_DIM
    if lax.axis_size("seq") == 4 and shape_fits:
        return two_chips(patches, w_qkv)
    return general(patches, w_qkv)


def solution(mesh):
    placed = (P(("groups", "seq"), None), P(None, None, "head"))
    return jax.shard_map(
        local, mesh=mesh, in_specs=placed, out_specs=P(("groups", "seq"), "head"), check_vma=False
    )
```

```python
import functools
import math

import jax
import jax.numpy as jnp
from jax import lax
from jax.experimental import pallas as pl
from jax.experimental.pallas import tpu as pltpu
from jax.sharding import PartitionSpec as P

D = 1024
HEAD_DIM = 64
COLS = 256
NEG_BIG = -1e30

STRIP = 16
BOTH = 2 * STRIP
PACK = 4

F32 = jnp.float32
BF16 = jnp.bfloat16


def shifted(block, axis, distance):
    devices = range(lax.axis_size(axis))
    route = [(i - distance, i) for i in devices if i - distance in devices]
    return lax.ppermute(block, axis, route)


def row_attention(queries, key_rows, value_rows, prev_keys, prev_values, first_row):
    row_count = queries.shape[1]
    scale = 1.0 / math.sqrt(HEAD_DIM)
    earlier_keys = jnp.concatenate([prev_keys[:, None], key_rows[:, :-1]], 1)
    earlier_values = jnp.concatenate([prev_values[:, None], value_rows[:, :-1]], 1)
    score_prev = (
        jnp.einsum("hrce,hrje->hrcj", queries, earlier_keys, preferred_element_type=jnp.float32)
        * scale
    )
    score_own = (
        jnp.einsum("hrce,hrje->hrcj", queries, key_rows, preferred_element_type=jnp.float32) * scale
    )
    column = lax.broadcasted_iota(jnp.int32, (1, 1, COLS, COLS), 2)
    slot = lax.broadcasted_iota(jnp.int32, (1, 1, COLS, COLS), 3)
    row_index = lax.broadcasted_iota(jnp.int32, (1, row_count, 1, 1), 1) + first_row
    allowed_prev = (slot > column) & (row_index > 0)
    allowed_own = slot <= column
    score_prev = jnp.where(allowed_prev, score_prev, NEG_BIG)
    score_own = jnp.where(allowed_own, score_own, NEG_BIG)
    highest = jnp.maximum(
        jnp.max(score_prev, axis=-1, keepdims=True), jnp.max(score_own, axis=-1, keepdims=True)
    )
    terms_prev = jnp.where(allowed_prev, jnp.exp(score_prev - highest), 0.0)
    terms_own = jnp.where(allowed_own, jnp.exp(score_own - highest), 0.0)
    totals = jnp.sum(terms_prev, axis=-1, keepdims=True) + jnp.sum(
        terms_own, axis=-1, keepdims=True
    )
    context = jnp.einsum(
        "hrcj,hrje->hrce",
        terms_prev.astype(jnp.bfloat16),
        earlier_values,
        preferred_element_type=jnp.float32,
    )
    context = context + jnp.einsum(
        "hrcj,hrje->hrce",
        terms_own.astype(jnp.bfloat16),
        value_rows,
        preferred_element_type=jnp.float32,
    )
    return context / totals


def column_attention(queries, key_rows, value_rows):
    row_count = queries.shape[1]
    scores = jnp.einsum(
        "hrce,hsce->hcrs", queries, key_rows, preferred_element_type=jnp.float32
    ) * (1.0 / math.sqrt(HEAD_DIM))
    later = lax.broadcasted_iota(jnp.int32, (1, 1, row_count, row_count), 2)
    earlier = lax.broadcasted_iota(jnp.int32, (1, 1, row_count, row_count), 3)
    allowed = earlier <= later
    scores = jnp.where(allowed, scores, NEG_BIG)
    highest = jnp.max(scores, axis=-1, keepdims=True)
    terms = jnp.where(allowed, jnp.exp(scores - highest), 0.0)
    totals = jnp.sum(terms, axis=-1, keepdims=True)
    context = jnp.einsum(
        "hcrs,hsce->hcre",
        terms.astype(jnp.bfloat16),
        value_rows,
        preferred_element_type=jnp.float32,
    )
    return jnp.transpose((context / totals).astype(jnp.bfloat16), (0, 2, 1, 3))


def general(patches, w_qkv):
    local_width = w_qkv.shape[2]
    head_count = local_width // HEAD_DIM
    row_count = patches.shape[0] // COLS
    weights_heads = w_qkv.reshape(D, 3, head_count, HEAD_DIM)
    projected = jnp.einsum(
        "td,dkhe->khte", patches, weights_heads, preferred_element_type=jnp.float32
    ).astype(jnp.bfloat16)
    prev_inputs = shifted(patches[-COLS:], "seq", 1)
    prev_pair = jnp.einsum(
        "td,dkhe->khte", prev_inputs, weights_heads[:, 1:], preferred_element_type=jnp.float32
    ).astype(jnp.bfloat16)
    first_row = lax.axis_index("seq") * row_count
    stacked = projected.reshape(3, head_count, row_count, COLS, HEAD_DIM)
    row_context = row_attention(
        stacked[0], stacked[1], stacked[2], prev_pair[0], prev_pair[1], first_row
    )
    column_pack = lax.all_to_all(stacked, "seq", split_axis=3, concat_axis=2, tiled=True)
    column_context = column_attention(column_pack[0], column_pack[1], column_pack[2])
    returned = lax.all_to_all(column_context, "seq", split_axis=1, concat_axis=2, tiled=True)
    mixed = (0.5 * (row_context + returned.astype(jnp.float32))).astype(jnp.bfloat16)
    return jnp.transpose(mixed, (1, 2, 0, 3)).reshape(row_count * COLS, local_width)


def iota(shape, axis):
    return lax.broadcasted_iota(jnp.int32, shape, axis)


def dot(left, right):
    return jnp.dot(left, right, preferred_element_type=F32)


def dot_t(left, right):
    return lax.dot_general(left, right, (((1,), (1,)), ((), ())), preferred_element_type=F32)


SLICES = 3
PIECES = 2
ANYWHERE = pl.BlockSpec(memory_space=pl.ANY)
ON_CHIP = pl.BlockSpec(memory_space=pltpu.VMEM)


def cost():
    return pl.CostEstimate(flops=1, bytes_accessed=1, transcendentals=0)


def params():
    return pltpu.CompilerParams(vmem_limit_bytes=28 << 20)


def started(copies):
    for copy in copies:
        copy.start()
    return copies


def finished(copies):
    for copy in copies:
        copy.wait()


def half_start(info, other, chunk, chunk_cols, offset):
    half = 1 - info[0] if other else info[0]
    return pl.multiple_of(half * (COLS // 2) + chunk * chunk_cols + offset, 16)


def project_kernel(info, x_ref, w_ref, *refs, chunk, chunk_cols, block, width):
    q_ref, k_ref, v_ref, mine_ref, other_ref, send_mine_ref, send_other_ref = refs[-7:]
    step = pl.program_id(0)
    steps = chunk_cols // block
    x = x_ref[...].reshape(STRIP * block, D)
    half = jnp.where(step < steps, info[0], 1 - info[0])
    offset = lax.rem(step, steps) * block
    start = pl.multiple_of(half * (COLS // 2) + chunk * chunk_cols + offset, block)
    rows = pl.ds(pl.multiple_of(offset, block), block)
    turned = []
    for i, natural_ref in enumerate((q_ref, k_ref, v_ref)):
        value = dot(x, w_ref[i]).astype(BF16).reshape(STRIP, block, width)
        natural_ref[:, pl.ds(start, block), :] = value
        turned.append(jnp.swapaxes(value, 0, 1))

    def store(triple_ref, send_ref):
        for i in range(3):
            triple_ref[i, rows] = turned[i]

        @pl.when(info[1] == 0)
        def _():
            send_ref[rows] = turned[2]

        @pl.when(info[1] == 1)
        def _():
            send_ref[rows] = turned[0]

    @pl.when(step < steps)
    def _():
        store(mine_ref, send_mine_ref)

    @pl.when(step >= steps)
    def _():
        store(other_ref, send_other_ref)


def project(info, x, w, natural, chunk, chunk_cols, block):
    width = w.shape[2]
    steps = chunk_cols // block
    natural_shape = jax.ShapeDtypeStruct((STRIP, COLS, width), BF16)
    triple = jax.ShapeDtypeStruct((3, chunk_cols, STRIP, width), BF16)
    single = jax.ShapeDtypeStruct((chunk_cols, STRIP, width), BF16)

    def x_map(j, info):
        half = jnp.where(j < steps, info[0], 1 - info[0])
        return (0, half * (COLS // 2 // block) + chunk * steps + lax.rem(j, steps), 0)

    operands = [x, w]
    in_specs = [
        pl.BlockSpec((STRIP, block, D), x_map),
        pl.BlockSpec(w.shape, lambda j, info: (0, 0, 0), pipeline_mode=pl.Buffered(1)),
    ]
    aliases = {}
    if natural is not None:
        aliases = {3: 0, 4: 1, 5: 2}
        operands += list(natural)
        in_specs += [ON_CHIP] * 3
    return pl.pallas_call(
        functools.partial(
            project_kernel, chunk=chunk, chunk_cols=chunk_cols, block=block, width=width
        ),
        out_shape=[natural_shape] * 3 + [triple, triple, single, single],
        grid_spec=pltpu.PrefetchScalarGridSpec(
            num_scalar_prefetch=1,
            grid=(2 * steps,),
            in_specs=in_specs,
            out_specs=[ON_CHIP] * 7,
        ),
        input_output_aliases=aliases,
        compiler_params=params(),
        cost_estimate=cost(),
        name="project",
    )(info, *operands)


def started(copies):
    for copy in copies:
        copy.start()
    return copies


def finished(copies):
    for copy in copies:
        copy.wait()


def half_start(info, other, chunk, chunk_cols):
    half = 1 - info[0] if other else info[0]
    return pl.multiple_of(half * (COLS // 2) + chunk * chunk_cols, chunk_cols)


def heads_of(shape, axis):
    return iota(shape, axis) // HEAD_DIM


def head_rows(rows_per_head, width):
    shape = (rows_per_head * (width // HEAD_DIM), width)
    own = iota(shape, 0) // rows_per_head == iota(shape, 1) // HEAD_DIM
    return jnp.where(own, 1.0 / math.sqrt(HEAD_DIM), 0.0).astype(BF16)


def row_kernel(info, *refs, width, top, rows):
    if top:
        halo_ref, w_ref = refs[:2]
    else:
        before_k_ref, before_v_ref = refs[:2]
    q_ref, k_ref, v_ref, out_ref, prev_k, prev_v = refs[2:]
    step = pl.program_id(0)
    heads = width // HEAD_DIM

    @pl.when(step == 0)
    def _():
        if top:
            prev_k[...] = dot(halo_ref[...], w_ref[1]).astype(BF16)
            prev_v[...] = dot(halo_ref[...], w_ref[2]).astype(BF16)
        else:
            prev_k[...] = before_k_ref[0]
            prev_v[...] = before_v_ref[0]

    own = iota((COLS, COLS), 1) <= iota((COLS, COLS), 0)
    lane_head = heads_of((COLS, width), 1)
    scale = 1.0 / math.sqrt(HEAD_DIM)
    spread = [jnp.where(lane_head == h, scale, 0.0).astype(BF16) for h in range(heads)]
    earlier_k, earlier_v = prev_k[...], prev_v[...]
    for r in range(rows):
        q, k, v = q_ref[r], k_ref[r], v_ref[r]
        result = None
        for h in range(heads):
            masked = q * spread[h]
            scores_prev = dot_t(masked, earlier_k)
            if top and r == 0:
                first = (step == 0) & (info[2] == 0)
                scores_prev = scores_prev + jnp.where(first, NEG_BIG, 0.0)
            scores = jnp.where(own, dot_t(masked, k), scores_prev)
            terms = jnp.exp(scores - jnp.max(scores, axis=1, keepdims=True))
            inverse = 1.0 / jnp.sum(terms, axis=1, keepdims=True)
            context = dot(jnp.where(own, terms, 0.0).astype(BF16), v)
            context = context + dot(jnp.where(own, 0.0, terms).astype(BF16), earlier_v)
            context = context * inverse
            result = context if h == 0 else jnp.where(lane_head == h, context, result)
        out_ref[r] = result
        earlier_k, earlier_v = k, v
    prev_k[...] = earlier_k
    prev_v[...] = earlier_v


def row_part(info, halo, w, q, k, v, first_row, row_count, rows=4):
    width = w.shape[2]
    top = first_row == 0
    steps = row_count // rows
    spec = pl.BlockSpec((rows, COLS, width), lambda r, info: (first_row // rows + r, 0, 0))
    if top:
        before = [halo, w]
        before_specs = [
            ON_CHIP,
            pl.BlockSpec(w.shape, lambda r, info: (0, 0, 0), pipeline_mode=pl.Buffered(1)),
        ]
    else:
        before = [k, v]
        before_specs = [pl.BlockSpec((1, COLS, width), lambda r, info: (first_row - 1, 0, 0))] * 2
    return pl.pallas_call(
        functools.partial(row_kernel, width=width, top=top, rows=rows),
        out_shape=jax.ShapeDtypeStruct((row_count, COLS, width), F32),
        grid_spec=pltpu.PrefetchScalarGridSpec(
            num_scalar_prefetch=1,
            grid=(steps,),
            in_specs=before_specs + [spec, spec, spec],
            out_specs=pl.BlockSpec((rows, COLS, width), lambda r, info: (r, 0, 0)),
            scratch_shapes=[
                pltpu.VMEM((COLS, width), BF16),
                pltpu.VMEM((COLS, width), BF16),
            ],
        ),
        compiler_params=params(),
        cost_estimate=cost(),
        name="row_attention",
    )(info, *before, q, k, v)


def column_of(mine, other, j):
    return jnp.concatenate([mine[j], other[j]], 0)


def scores_of(keys, queries, spread, heads):
    return dot_t(keys, jnp.concatenate([queries] * heads, 0) * spread)


def later_key(core, heads):
    shape = (BOTH, heads * BOTH)
    key_row = (iota(shape, 0) + STRIP * core) & (BOTH - 1)
    query_row = (iota(shape, 1) + STRIP * core) & (BOTH - 1)
    return key_row > query_row


def arriving(arrays, buffers, sems, cols):
    step = cols // PIECES
    pieces = []
    for p in range(PIECES):
        part = pl.ds(p * step, step)
        copies = []
        for n, ((ref, axis, first), buffer) in enumerate(zip(arrays, buffers)):
            width = ref.shape[axis] // PIECES
            at = (slice(None),) * axis + (pl.ds(p * width, width),)
            source = (pl.ds(first, buffer.shape[0]),) + at[1:] if axis else at
            copies.append(
                pltpu.make_async_copy(ref.at[source], buffer.at[at], sems.at[n, p])
            )
        pieces.append(started(copies))
    return pieces


def piecewise(pieces, cols, body):
    groups = cols // PACK // PIECES
    for p, copies in enumerate(pieces):
        finished(copies)
        lax.fori_loop(p * groups, (p + 1) * groups, body, 0, unroll=4)


def buffers_for(shapes):
    buffers = [pltpu.VMEM(shape, dtype) for shape, dtype in shapes]
    return buffers + [pltpu.SemaphoreType.DMA((len(shapes), PIECES))]


def maxima_kernel(info, *refs, heads, cols, chunks):
    in_refs, out_ref, buffers, sems = refs[: 2 * chunks], refs[-3], refs[-2], refs[-1]
    hidden = later_key(info[0], heads)
    spread = head_rows(BOTH, heads * HEAD_DIM)

    @pl.when(info[1] == 1)
    def _():
        copies = [
            pltpu.make_async_copy(in_refs[2 * c].at[pl.ds(0, 2)], buffers.at[c], sems.at[c])
            for c in range(chunks)
        ]
        started(copies)
        for c in range(chunks):
            other_ref = in_refs[2 * c + 1]
            copies[c].wait()

            def body(g, carry):
                part = pl.ds(g * PACK, PACK)
                qm, qo = buffers[c, 0, part], other_ref[0, part]
                km, ko = buffers[c, 1, part], other_ref[1, part]
                tops = []
                for j in range(PACK):
                    scores = scores_of(column_of(km, ko, j), column_of(qm, qo, j), spread, heads)
                    tops.append(jnp.max(jnp.where(hidden, NEG_BIG, scores), axis=0, keepdims=True))
                out_ref[c, part] = jnp.concatenate(tops, 0)
                return carry

            lax.fori_loop(0, cols // PACK, body, 0, unroll=4)


def maxima(info, mine, other):
    _, cols, _, width = mine[0].shape
    heads = width // HEAD_DIM
    chunks = len(mine)
    return pl.pallas_call(
        functools.partial(maxima_kernel, heads=heads, cols=cols, chunks=chunks),
        out_shape=jax.ShapeDtypeStruct((chunks, cols, heads * BOTH), F32),
        grid_spec=pltpu.PrefetchScalarGridSpec(
            num_scalar_prefetch=1,
            grid=(),
            in_specs=[ANYWHERE, ON_CHIP] * chunks,
            out_specs=ON_CHIP,
            scratch_shapes=[
                pltpu.VMEM((chunks, 2, cols, STRIP, width), BF16),
                pltpu.SemaphoreType.DMA((chunks,)),
            ],
        ),
        compiler_params=params(),
        cost_estimate=cost(),
        name="maxima",
    )(info, *[array for pair in zip(mine, other) for array in pair])


def weights_kernel(info, *refs, heads, cols, chunk):
    qm_ref, qo_ref, mine_ref, other_ref, top_ref, w_ref, stats, km_buf, sems = refs
    spread = head_rows(BOTH, heads * HEAD_DIM)

    def body(g, carry):
        part = pl.ds(g * PACK, PACK)
        qm, qo = qm_ref[part], qo_ref[part]
        km, ko = km_buf[0, part], other_ref[1, part]
        below = top_ref[chunk, part]
        tops, totals, turned = [], [], []
        for j in range(PACK):
            scores = scores_of(column_of(km, ko, j), column_of(qm, qo, j), spread, heads)
            top = jnp.maximum(jnp.max(scores, axis=0, keepdims=True), below[j : j + 1])
            terms = jnp.exp(scores - top)
            tops.append(top)
            totals.append(jnp.sum(terms, axis=0, keepdims=True))
            turned.append(terms)
        w_ref[g] = jnp.concatenate(turned, 0).T.astype(BF16)
        stats[0, part] = jnp.concatenate(tops, 0)
        stats[1, part] = jnp.concatenate(totals, 0)
        return carry

    @pl.when(info[1] == 0)
    def _():
        piecewise(arriving([(mine_ref, 1, 1)], [km_buf], sems, cols), cols, body)
        rest = stats[...].reshape(2 * cols, heads * BOTH)
        for n in range(SLICES):
            part = rest.astype(BF16)
            w_ref[cols // PACK + n] = part
            rest = rest - part.astype(F32)


def cross_weights(info, recv_mine, recv_other, mine, other, top, chunk):
    _, cols, _, width = mine.shape
    heads = width // HEAD_DIM
    rows = heads * BOTH
    keys = ((1, cols, STRIP, width), BF16)
    return pl.pallas_call(
        functools.partial(weights_kernel, heads=heads, cols=cols, chunk=chunk),
        out_shape=jax.ShapeDtypeStruct((cols // PACK + SLICES, rows, PACK * BOTH), BF16),
        grid_spec=pltpu.PrefetchScalarGridSpec(
            num_scalar_prefetch=1,
            grid=(),
            in_specs=[ON_CHIP, ON_CHIP, ANYWHERE, ON_CHIP, ON_CHIP],
            out_specs=ON_CHIP,
            scratch_shapes=[pltpu.VMEM((2, cols, rows), F32)] + buffers_for([keys]),
        ),
        compiler_params=params(),
        cost_estimate=cost(),
        name="cross_weights",
    )(info, recv_mine, recv_other, mine, other, top)


def column_kernel(info, *refs, heads, cols):
    mine_ref, other_buf, vm_buf, vo_buf, w_buf = refs[:5]
    om_ref, oo_ref, stats, mine_buf, sems = refs[5:]
    hidden = later_key(info[0], heads)
    width = heads * HEAD_DIM
    rows = heads * BOTH
    spread = head_rows(BOTH, width)
    lower = info[1] == 1
    pair = 2 * BOTH
    keys = PACK * BOTH
    key_column = (iota((1, 2 * keys), 1) & (keys - 1)) // BOTH
    picks = [jnp.where(key_column == j, 1.0, 0.0).astype(BF16) for j in range(PACK)]
    left_head = iota((BOTH, 2 * HEAD_DIM), 1) < HEAD_DIM

    def body(g, carry):
        part = pl.ds(g * PACK, PACK)
        qm, qo = mine_buf[0, part], other_buf[0, part]
        km, ko = mine_buf[1, part], other_buf[1, part]
        above, far_totals = stats[0, part], stats[1, part]
        totals, turned = [], []
        for j in range(PACK):
            scores = scores_of(column_of(km, ko, j), column_of(qm, qo, j), spread, heads)
            scores = jnp.where(hidden, NEG_BIG, scores)
            top = jnp.max(scores, axis=0, keepdims=True)
            top = jnp.where(lower, above[j : j + 1], top)
            terms = jnp.exp(scores - top)
            totals.append(jnp.sum(terms, axis=0, keepdims=True))
            turned.append(terms)
        inverse = 1.0 / (jnp.concatenate(totals, 0) + far_totals)
        inverse = jnp.concatenate([inverse, inverse], 0).T
        near = jnp.concatenate(turned, 0).T.astype(BF16)
        weights = jnp.concatenate([near, w_buf[g]], 1)
        near_v = [column_of(mine_buf[2, part], other_buf[2, part], j) for j in range(PACK)]
        far_v = [column_of(vm_buf[part], vo_buf[part], j) for j in range(PACK)]
        values = jnp.concatenate(near_v + far_v, 0)
        left = jnp.concatenate([weights * picks[j] for j in range(PACK)], 0)
        context = dot(left, values)
        for j in range(PACK):
            outs = []
            for t in range(heads // 2):
                lanes = slice(t * 2 * HEAD_DIM, (t + 1) * 2 * HEAD_DIM)
                at = j * rows + t * pair
                first = t * pair
                out = jnp.where(
                    left_head,
                    context[at : at + BOTH, lanes],
                    context[at + BOTH : at + 2 * BOTH, lanes],
                )
                factor = jnp.where(
                    left_head,
                    inverse[first : first + BOTH, j : j + 1],
                    inverse[first + BOTH : first + 2 * BOTH, j : j + 1],
                )
                outs.append((out * factor).astype(BF16))
            out = jnp.concatenate(outs, 1)
            om_ref[g * PACK + j] = out[:STRIP]
            oo_ref[g * PACK + j] = out[STRIP:]
        return carry

    pieces = arriving([(mine_ref, 1, 0)], [mine_buf], sems, cols)
    whole = w_buf[cols // PACK].astype(F32)
    for n in range(1, SLICES):
        whole = whole + w_buf[cols // PACK + n].astype(F32)
    stats[...] = whole.reshape(stats.shape)
    piecewise(pieces, cols, body)


def column_part(info, mine, other, recv_mine, recv_other, weights):
    _, cols, _, width = mine.shape
    heads = width // HEAD_DIM
    operands = [mine, other, recv_mine, recv_other, weights]
    shape = jax.ShapeDtypeStruct((cols, STRIP, width), BF16)
    return pl.pallas_call(
        functools.partial(column_kernel, heads=heads, cols=cols),
        out_shape=[shape, shape],
        grid_spec=pltpu.PrefetchScalarGridSpec(
            num_scalar_prefetch=1,
            grid=(),
            in_specs=[ANYWHERE] + [ON_CHIP] * 4,
            out_specs=[ON_CHIP] * 2,
            scratch_shapes=[pltpu.VMEM((2, cols, heads * BOTH), F32)]
            + buffers_for([(mine.shape, mine.dtype)]),
        ),
        compiler_params=params(),
        cost_estimate=cost(),
        name="column_attention",
    )(info, *operands)


def mix_kernel(info, *refs, chunk, cols, parts):
    row_refs, pair_refs = refs[:parts], refs[parts : parts + 2]
    out_ref, row_buf, near_buf, out_buf, row_sem, near_sem, out_sem = refs[-7:]
    copies = []
    for o in range(2):
        span = pl.ds(half_start(info, o == 1, chunk, cols), cols)
        group = []
        if o == 0:
            group = [pltpu.make_async_copy(pair_refs[0], near_buf, near_sem)]
        at = 0
        for n, row_ref in enumerate(row_refs):
            rows = pl.ds(at, row_ref.shape[0])
            group.append(
                pltpu.make_async_copy(
                    row_ref.at[:, span, :], row_buf.at[o, rows], row_sem.at[o, n]
                )
            )
            at += row_ref.shape[0]
        copies.append((span, started(group)))
    out_copies = []
    for o in range(2):
        span, group = copies[o]
        finished(group)
        column = near_buf[...] if o == 0 else pair_refs[1][...]
        column = jnp.swapaxes(column, 0, 1).astype(F32)
        out_buf[o] = (0.5 * (row_buf[o] + column)).astype(BF16)
        out_copies += started(
            [pltpu.make_async_copy(out_buf.at[o], out_ref.at[:, span, :], out_sem.at[o])]
        )
    finished(out_copies)


def mix(info, row_context, mine, other, done, chunk):
    cols, _, width = mine.shape
    parts = len(row_context)
    operands = list(row_context) + [mine, other]
    aliases = {}
    if done is not None:
        operands.append(done)
        aliases = {len(operands): 0}
    return pl.pallas_call(
        functools.partial(mix_kernel, chunk=chunk, cols=cols, parts=parts),
        out_shape=jax.ShapeDtypeStruct((STRIP, COLS, width), BF16),
        grid_spec=pltpu.PrefetchScalarGridSpec(
            num_scalar_prefetch=1,
            grid=(),
            in_specs=[ON_CHIP if n == parts + 1 else ANYWHERE for n in range(len(operands))],
            out_specs=ANYWHERE,
            scratch_shapes=[
                pltpu.VMEM((2, STRIP, cols, width), F32),
                pltpu.VMEM((cols, STRIP, width), BF16),
                pltpu.VMEM((2, STRIP, cols, width), BF16),
                pltpu.SemaphoreType.DMA((2, parts)),
                pltpu.SemaphoreType.DMA,
                pltpu.SemaphoreType.DMA((2,)),
            ],
        ),
        input_output_aliases=aliases,
        compiler_params=params(),
        cost_estimate=cost(),
        name="mix",
    )(info, *operands)


CORE_SWAP = [(0, 1), (1, 0), (2, 3), (3, 2)]
SAME_CORE = [(0, 2), (1, 3), (2, 0), (3, 1)]
OTHER_CORE = [(0, 3), (1, 2), (2, 1), (3, 0)]
DOWN_SAME = [(0, 2), (1, 3)]
UP_SAME = [(2, 0), (3, 1)]


def send(block, route):
    return pltpu.with_memory_space_constraint(lax.ppermute(block, "seq", route), pltpu.VMEM)


def in_hbm(array):
    return pltpu.with_memory_space_constraint(array, pltpu.HBM)


def after(value, *earlier):
    return lax.optimization_barrier((value,) + earlier)[0]


def two_chips(patches, w_qkv):
    width = w_qkv.shape[2]
    chunks = 2
    chunk_cols = COLS // 2 // chunks
    seq = lax.axis_index("seq")
    info = jnp.stack([seq % 2, seq // 2, seq]).astype(jnp.int32)
    halo = send(patches[-COLS:], [(0, 1), (1, 2), (2, 3)])
    x = patches.reshape(STRIP, COLS, D)
    w = jnp.transpose(w_qkv, (1, 0, 2))

    first = project(info, in_hbm(x), in_hbm(w), None, 0, chunk_cols, 32)
    info = after(info, halo)
    second = project(info, x, w, first[:3], 1, chunk_cols, 32)
    natural = second[:3]
    mine = [first[3], second[3]]
    other = [send(first[4], CORE_SWAP), send(second[4], CORE_SWAP)]
    received = [(send(first[5], SAME_CORE), send(first[6], OTHER_CORE))]

    rows_top = row_part(info, halo, w, *natural, 0, 8)
    info = after(info, rows_top)
    top = maxima(info, mine, other)
    below = send(top, UP_SAME)
    info = after(info, top)
    rows_mid = row_part(info, halo, w, *natural, 8, 4)
    held = [after(part, rows_mid) for part in second[5:7]]
    received.append((send(held[0], SAME_CORE), send(held[1], OTHER_CORE)))
    info = after(info, rows_mid)
    far = []
    for c in range(chunks):
        weights = cross_weights(info, *received[c], mine[c], other[c], below, c)
        info = after(info, weights)
        far.append(send(weights, DOWN_SAME))
        if c == 0:
            rows_low = row_part(info, halo, w, *natural, 12, 4)
            row_context = (rows_top, rows_mid, rows_low)
            info = after(info, rows_low)
    out = None
    for c in range(chunks):
        near, remote = column_part(info, mine[c], other[c], *received[c], far[c])
        remote = send(remote, CORE_SWAP)
        info = after(info, near)
        out = mix(info, row_context, near, remote, out, c)
    return out.reshape(STRIP * COLS, width)


def local(patches, w_qkv):
    shape_fits = patches.shape[0] == STRIP * COLS and w_qkv.shape[2] == 4 * HEAD_DIM
    if lax.axis_size("seq") == 4 and shape_fits:
        return two_chips(patches, w_qkv)
    return general(patches, w_qkv)


def solution(mesh):
    placed = (P(("groups", "seq"), None), P(None, None, "head"))
    return jax.shard_map(
        local, mesh=mesh, in_specs=placed, out_specs=P(("groups", "seq"), "head"), check_vma=False
    )
```

```python
import functools
import math

import jax
import jax.numpy as jnp
from jax import lax
from jax.experimental import pallas as pl
from jax.experimental.pallas import tpu as pltpu
from jax.sharding import PartitionSpec as P

D = 1024
HEAD_DIM = 64
COLS = 256
NEG_BIG = -1e30

STRIP = 16
BOTH = 2 * STRIP
PACK = 4

F32 = jnp.float32
BF16 = jnp.bfloat16


def shifted(block, axis, distance):
    devices = range(lax.axis_size(axis))
    route = [(i - distance, i) for i in devices if i - distance in devices]
    return lax.ppermute(block, axis, route)


def row_attention(queries, key_rows, value_rows, prev_keys, prev_values, first_row):
    row_count = queries.shape[1]
    scale = 1.0 / math.sqrt(HEAD_DIM)
    earlier_keys = jnp.concatenate([prev_keys[:, None], key_rows[:, :-1]], 1)
    earlier_values = jnp.concatenate([prev_values[:, None], value_rows[:, :-1]], 1)
    score_prev = (
        jnp.einsum("hrce,hrje->hrcj", queries, earlier_keys, preferred_element_type=jnp.float32)
        * scale
    )
    score_own = (
        jnp.einsum("hrce,hrje->hrcj", queries, key_rows, preferred_element_type=jnp.float32) * scale
    )
    column = lax.broadcasted_iota(jnp.int32, (1, 1, COLS, COLS), 2)
    slot = lax.broadcasted_iota(jnp.int32, (1, 1, COLS, COLS), 3)
    row_index = lax.broadcasted_iota(jnp.int32, (1, row_count, 1, 1), 1) + first_row
    allowed_prev = (slot > column) & (row_index > 0)
    allowed_own = slot <= column
    score_prev = jnp.where(allowed_prev, score_prev, NEG_BIG)
    score_own = jnp.where(allowed_own, score_own, NEG_BIG)
    highest = jnp.maximum(
        jnp.max(score_prev, axis=-1, keepdims=True), jnp.max(score_own, axis=-1, keepdims=True)
    )
    terms_prev = jnp.where(allowed_prev, jnp.exp(score_prev - highest), 0.0)
    terms_own = jnp.where(allowed_own, jnp.exp(score_own - highest), 0.0)
    totals = jnp.sum(terms_prev, axis=-1, keepdims=True) + jnp.sum(
        terms_own, axis=-1, keepdims=True
    )
    context = jnp.einsum(
        "hrcj,hrje->hrce",
        terms_prev.astype(jnp.bfloat16),
        earlier_values,
        preferred_element_type=jnp.float32,
    )
    context = context + jnp.einsum(
        "hrcj,hrje->hrce",
        terms_own.astype(jnp.bfloat16),
        value_rows,
        preferred_element_type=jnp.float32,
    )
    return context / totals


def column_attention(queries, key_rows, value_rows):
    row_count = queries.shape[1]
    scores = jnp.einsum(
        "hrce,hsce->hcrs", queries, key_rows, preferred_element_type=jnp.float32
    ) * (1.0 / math.sqrt(HEAD_DIM))
    later = lax.broadcasted_iota(jnp.int32, (1, 1, row_count, row_count), 2)
    earlier = lax.broadcasted_iota(jnp.int32, (1, 1, row_count, row_count), 3)
    allowed = earlier <= later
    scores = jnp.where(allowed, scores, NEG_BIG)
    highest = jnp.max(scores, axis=-1, keepdims=True)
    terms = jnp.where(allowed, jnp.exp(scores - highest), 0.0)
    totals = jnp.sum(terms, axis=-1, keepdims=True)
    context = jnp.einsum(
        "hcrs,hsce->hcre",
        terms.astype(jnp.bfloat16),
        value_rows,
        preferred_element_type=jnp.float32,
    )
    return jnp.transpose((context / totals).astype(jnp.bfloat16), (0, 2, 1, 3))


def general(patches, w_qkv):
    local_width = w_qkv.shape[2]
    head_count = local_width // HEAD_DIM
    row_count = patches.shape[0] // COLS
    weights_heads = w_qkv.reshape(D, 3, head_count, HEAD_DIM)
    projected = jnp.einsum(
        "td,dkhe->khte", patches, weights_heads, preferred_element_type=jnp.float32
    ).astype(jnp.bfloat16)
    prev_inputs = shifted(patches[-COLS:], "seq", 1)
    prev_pair = jnp.einsum(
        "td,dkhe->khte", prev_inputs, weights_heads[:, 1:], preferred_element_type=jnp.float32
    ).astype(jnp.bfloat16)
    first_row = lax.axis_index("seq") * row_count
    stacked = projected.reshape(3, head_count, row_count, COLS, HEAD_DIM)
    row_context = row_attention(
        stacked[0], stacked[1], stacked[2], prev_pair[0], prev_pair[1], first_row
    )
    column_pack = lax.all_to_all(stacked, "seq", split_axis=3, concat_axis=2, tiled=True)
    column_context = column_attention(column_pack[0], column_pack[1], column_pack[2])
    returned = lax.all_to_all(column_context, "seq", split_axis=1, concat_axis=2, tiled=True)
    mixed = (0.5 * (row_context + returned.astype(jnp.float32))).astype(jnp.bfloat16)
    return jnp.transpose(mixed, (1, 2, 0, 3)).reshape(row_count * COLS, local_width)


def iota(shape, axis):
    return lax.broadcasted_iota(jnp.int32, shape, axis)


def dot(left, right):
    return jnp.dot(left, right, preferred_element_type=F32)


def dot_t(left, right):
    return lax.dot_general(left, right, (((1,), (1,)), ((), ())), preferred_element_type=F32)


SLICES = 3
HALF = COLS // 2
ANYWHERE = pl.BlockSpec(memory_space=pl.ANY)
ON_CHIP = pl.BlockSpec(memory_space=pltpu.VMEM)


def call(kernel, info, operands, out_shape, scratch=(), **more):
    options = dict(
        in_specs=[ON_CHIP] * len(operands),
        out_specs=jax.tree.map(lambda _: ON_CHIP, out_shape),
    )
    aliases = more.pop("aliases", {})
    name = more.pop("name")
    flops = more.pop("flops", 1)
    options.update(more)
    return pl.pallas_call(
        kernel,
        out_shape=out_shape,
        grid_spec=pltpu.PrefetchScalarGridSpec(
            num_scalar_prefetch=1,
            grid=options.pop("grid", ()),
            scratch_shapes=list(scratch),
            **options,
        ),
        input_output_aliases=aliases,
        compiler_params=pltpu.CompilerParams(vmem_limit_bytes=28 << 20),
        cost_estimate=pl.CostEstimate(flops=flops, bytes_accessed=1, transcendentals=0),
        name=name,
    )(info, *operands)


def column_span(info, other, first, cols):
    half = 1 - info[0] if other else info[0]
    return pl.ds(pl.multiple_of(half * HALF + first, 16), cols)


def sent_slot(info):
    return jnp.where(info[1] == 0, 2, 0)


def projected(x, w, natural_ref, last_ref, turned_refs, slot, columns, rows):
    _, block, depth = x.shape
    part = STRIP // 2
    parts = [
        dot(x[r : r + part].reshape(part * block, depth), w).astype(BF16) for r in (0, part)
    ]
    value = jnp.concatenate(parts, 0).reshape(STRIP, block, w.shape[1])
    natural_ref[slot, :, columns, :] = value

    @pl.when(slot > 0)
    def _():
        last_ref[slot - 1, columns, :] = value[STRIP - 1]

    turned = jnp.swapaxes(value, 0, 1)
    for ref in turned_refs:
        ref[rows] = turned


def first_kernel(info, x_ref, w_ref, *refs, block):
    natural_ref, mine_ref, other_ref, last_ref, send_mine_ref, send_other_ref, x_out = refs[:7]
    w_buf, x_sem, w_sem = refs[7:]
    slot = sent_slot(info)
    w_copy = pltpu.make_async_copy(w_ref.at[slot], w_buf, w_sem)
    w_copy.start()
    pieces = []
    for other in (False, True):
        for first in range(0, HALF, block):
            columns = column_span(info, other, first, block)
            copy = pltpu.make_async_copy(
                x_ref.at[:, columns, :], x_out.at[:, columns, :], x_sem.at[len(pieces)]
            )
            copy.start()
            pieces.append((copy, other, first, columns))
    w_copy.wait()
    w = w_buf[...]
    for copy, other, first, columns in pieces:
        copy.wait()
        triple_ref = other_ref if other else mine_ref
        send_ref = send_other_ref if other else send_mine_ref
        projected(
            x_out[:, columns, :],
            w,
            natural_ref,
            last_ref,
            (triple_ref.at[slot], send_ref),
            slot,
            columns,
            pl.ds(first, block),
        )


def rest_kernel(info, x_ref, w_ref, *refs, block):
    natural_ref, mine_ref, other_ref, last_ref = refs[-4:]
    for slot in (2 - sent_slot(info), 1):
        w = w_ref[slot]
        for other, triple_ref in ((False, mine_ref), (True, other_ref)):
            for first in range(0, HALF, block):
                columns = column_span(info, other, first, block)
                projected(
                    x_ref[:, columns, :],
                    w,
                    natural_ref,
                    last_ref,
                    (triple_ref.at[slot],),
                    slot,
                    columns,
                    pl.ds(first, block),
                )


def project(info, x, w, block=64):
    width = w.shape[2]
    natural = jax.ShapeDtypeStruct((3, STRIP, COLS, width), BF16)
    triple = jax.ShapeDtypeStruct((3, HALF, STRIP, width), BF16)
    last = jax.ShapeDtypeStruct((2, COLS, width), BF16)
    single = jax.ShapeDtypeStruct((HALF, STRIP, width), BF16)
    return call(
        functools.partial(first_kernel, block=block),
        info,
        [x, w],
        [natural, triple, triple, last, single, single, jax.ShapeDtypeStruct(x.shape, BF16)],
        [
            pltpu.VMEM(w.shape[1:], BF16),
            pltpu.SemaphoreType.DMA((COLS // block,)),
            pltpu.SemaphoreType.DMA,
        ],
        in_specs=[ANYWHERE] * 2,
        name="project_sent",
    )


def project_rest(info, x, w, kept, block=64):
    return call(
        functools.partial(rest_kernel, block=block),
        info,
        [x, w] + list(kept),
        [jax.ShapeDtypeStruct(array.shape, BF16) for array in kept],
        aliases={3 + n: n for n in range(len(kept))},
        name="project_rest",
    )


def heads_of(shape, axis):
    return iota(shape, axis) // HEAD_DIM


def head_rows(rows_per_head, width):
    shape = (rows_per_head * (width // HEAD_DIM), width)
    own = iota(shape, 0) // rows_per_head == iota(shape, 1) // HEAD_DIM
    return jnp.where(own, 1.0 / math.sqrt(HEAD_DIM), 0.0).astype(BF16)


def row_kernel(info, *refs, width, top, rows):
    before_k_ref, before_v_ref, q_ref, k_ref, v_ref, out_ref, prev_k, prev_v = refs
    step = pl.program_id(0)
    heads = width // HEAD_DIM

    @pl.when(step == 0)
    def _():
        prev_k[...] = before_k_ref[0] if top else before_k_ref[0, 0]
        prev_v[...] = before_v_ref[0] if top else before_v_ref[0, 0]

    own = iota((COLS, COLS), 1) <= iota((COLS, COLS), 0)
    lane_head = heads_of((COLS, width), 1)
    scale = 1.0 / math.sqrt(HEAD_DIM)
    spread = [jnp.where(lane_head == h, scale, 0.0).astype(BF16) for h in range(heads)]
    earlier_k, earlier_v = prev_k[...], prev_v[...]
    for r in range(rows):
        q, k, v = q_ref[0, r], k_ref[0, r], v_ref[0, r]
        result = None
        for h in range(heads):
            masked = q * spread[h]
            scores_prev = dot_t(masked, earlier_k)
            if top and r == 0:
                first = (step == 0) & (info[2] == 0)
                scores_prev = scores_prev + jnp.where(first, NEG_BIG, 0.0)
            scores = jnp.where(own, dot_t(masked, k), scores_prev)
            terms = jnp.exp(scores - jnp.max(scores, axis=1, keepdims=True))
            inverse = 1.0 / jnp.sum(terms, axis=1, keepdims=True)
            context = dot(jnp.where(own, terms, 0.0).astype(BF16), v)
            context = context + dot(jnp.where(own, 0.0, terms).astype(BF16), earlier_v)
            context = context * inverse
            result = context if h == 0 else jnp.where(lane_head == h, context, result)
        out_ref[r] = result
        earlier_k, earlier_v = k, v
    prev_k[...] = earlier_k
    prev_v[...] = earlier_v


def row_part(info, halo, natural, first_row, row_count, rows=4):
    width = natural.shape[3]
    top = first_row == 0
    block = (1, rows, COLS, width)

    def spec(slot):
        return pl.BlockSpec(block, lambda r, info: (slot, first_row // rows + r, 0, 0))

    def before_spec(slot):
        if top:
            return pl.BlockSpec((1, COLS, width), lambda r, info: (slot - 1, 0, 0))
        return pl.BlockSpec((1, 1, COLS, width), lambda r, info: (slot, first_row - 1, 0, 0))

    return call(
        functools.partial(row_kernel, width=width, top=top, rows=rows),
        info,
        [halo if top else natural] * 2 + [natural] * 3,
        jax.ShapeDtypeStruct((row_count, COLS, width), F32),
        [pltpu.VMEM((COLS, width), BF16)] * 2,
        grid=(row_count // rows,),
        in_specs=[before_spec(1), before_spec(2)] + [spec(slot) for slot in range(3)],
        out_specs=pl.BlockSpec((rows, COLS, width), lambda r, info: (r, 0, 0)),
        flops=2 * 10**10,
        name="row_attention",
    )


def column_of(mine, other, j):
    return jnp.concatenate([mine[j], other[j]], 0)


def scores_of(keys, queries, spread, heads):
    return dot_t(keys, jnp.concatenate([queries] * heads, 0) * spread)


def later_key(core, heads):
    shape = (BOTH, heads * BOTH)
    key_row = (iota(shape, 0) + STRIP * core) & (BOTH - 1)
    query_row = (iota(shape, 1) + STRIP * core) & (BOTH - 1)
    return key_row > query_row


def by_pack(first, count, body):
    def run(g, carry):
        body(g, pl.ds(first + g * PACK, PACK))
        return carry

    lax.fori_loop(0, count // PACK, run, 0, unroll=4)


def maxima_kernel(info, mine_ref, other_ref, out_ref, *, heads):
    hidden = later_key(info[0], heads)
    spread = head_rows(BOTH, heads * HEAD_DIM)

    def body(g, part):
        qm, qo = mine_ref[0, part], other_ref[0, part]
        km, ko = mine_ref[1, part], other_ref[1, part]
        tops = []
        for j in range(PACK):
            scores = scores_of(column_of(km, ko, j), column_of(qm, qo, j), spread, heads)
            tops.append(jnp.max(jnp.where(hidden, NEG_BIG, scores), axis=0, keepdims=True))
        out_ref[part] = jnp.concatenate(tops, 0)

    @pl.when(info[1] == 1)
    def _():
        by_pack(0, mine_ref.shape[1], body)


def maxima(info, mine, other):
    heads = mine.shape[-1] // HEAD_DIM
    return call(
        functools.partial(maxima_kernel, heads=heads),
        info,
        [mine, other],
        jax.ShapeDtypeStruct((mine.shape[1], heads * BOTH), F32),
        name="maxima",
    )


def weights_kernel(
    info, qm_ref, qo_ref, mine_ref, other_ref, top_ref, w_ref, stats, *, heads, first, cols
):
    spread = head_rows(BOTH, heads * HEAD_DIM)

    def body(g, part):
        qm, qo = qm_ref[part], qo_ref[part]
        km, ko = mine_ref[1, part], other_ref[1, part]
        below = top_ref[part]
        tops, totals, turned = [], [], []
        for j in range(PACK):
            scores = scores_of(column_of(km, ko, j), column_of(qm, qo, j), spread, heads)
            top = jnp.maximum(jnp.max(scores, axis=0, keepdims=True), below[j : j + 1])
            terms = jnp.exp(scores - top)
            tops.append(top)
            totals.append(jnp.sum(terms, axis=0, keepdims=True))
            turned.append(terms)
        w_ref[pl.ds(g * heads * BOTH, heads * BOTH)] = jnp.concatenate(turned, 0).T.astype(BF16)
        stats[0, pl.ds(g * PACK, PACK)] = jnp.concatenate(tops, 0)
        stats[1, pl.ds(g * PACK, PACK)] = jnp.concatenate(totals, 0)

    @pl.when(info[1] == 0)
    def _():
        by_pack(first, cols, body)
        rest = stats[...].reshape(2 * cols, heads * BOTH)
        at = cols // PACK * heads * BOTH
        for n in range(SLICES):
            part = rest.astype(BF16)
            w_ref[at + n * 2 * cols : at + (n + 1) * 2 * cols] = part
            rest = rest - part.astype(F32)


def cross_weights(info, recv_mine, recv_other, mine, other, top, first, cols):
    heads = mine.shape[-1] // HEAD_DIM
    rows = heads * BOTH
    return call(
        functools.partial(weights_kernel, heads=heads, first=first, cols=cols),
        info,
        [recv_mine, recv_other, mine, other, top],
        jax.ShapeDtypeStruct((cols // PACK * rows + SLICES * 2 * cols, PACK * BOTH), BF16),
        [pltpu.VMEM((2, cols, rows), F32)],
        name="cross_weights",
    )


def column_kernel(
    info, mine_ref, other_ref, vm_ref, vo_ref, w_ref, om_ref, oo_ref, stats, *, heads, first, cols
):
    hidden = later_key(info[0], heads)
    width = heads * HEAD_DIM
    rows = heads * BOTH
    spread = head_rows(BOTH, width)
    lower = info[1] == 1
    pair = 2 * BOTH
    keys = PACK * BOTH
    key_column = (iota((1, 2 * keys), 1) & (keys - 1)) // BOTH
    picks = [jnp.where(key_column == j, 1.0, 0.0).astype(BF16) for j in range(PACK)]
    left_head = iota((BOTH, 2 * HEAD_DIM), 1) < HEAD_DIM
    at = cols // PACK * rows
    whole = w_ref[at : at + 2 * cols].astype(F32)
    for n in range(1, SLICES):
        whole = whole + w_ref[at + n * 2 * cols : at + (n + 1) * 2 * cols].astype(F32)
    stats[...] = whole.reshape(stats.shape)

    def body(g, part):
        local = pl.ds(g * PACK, PACK)
        qm, qo = mine_ref[0, part], other_ref[0, part]
        km, ko = mine_ref[1, part], other_ref[1, part]
        above, far_totals = stats[0, local], stats[1, local]
        totals, turned = [], []
        for j in range(PACK):
            scores = scores_of(column_of(km, ko, j), column_of(qm, qo, j), spread, heads)
            scores = jnp.where(hidden, NEG_BIG, scores)
            top = jnp.max(scores, axis=0, keepdims=True)
            top = jnp.where(lower, above[j : j + 1], top)
            terms = jnp.exp(scores - top)
            totals.append(jnp.sum(terms, axis=0, keepdims=True))
            turned.append(terms)
        inverse = 1.0 / (jnp.concatenate(totals, 0) + far_totals)
        inverse = jnp.concatenate([inverse, inverse], 0).T
        near = jnp.concatenate(turned, 0).T.astype(BF16)
        weights = jnp.concatenate([near, w_ref[pl.ds(g * rows, rows)]], 1)
        near_v = [column_of(mine_ref[2, part], other_ref[2, part], j) for j in range(PACK)]
        far_v = [column_of(vm_ref[part], vo_ref[part], j) for j in range(PACK)]
        values = jnp.concatenate(near_v + far_v, 0)
        left = jnp.concatenate([weights * picks[j] for j in range(PACK)], 0)
        context = dot(left, values)
        for j in range(PACK):
            outs = []
            for t in range(heads // 2):
                lanes = slice(t * 2 * HEAD_DIM, (t + 1) * 2 * HEAD_DIM)
                at = j * rows + t * pair
                head = t * pair
                out = jnp.where(
                    left_head,
                    context[at : at + BOTH, lanes],
                    context[at + BOTH : at + 2 * BOTH, lanes],
                )
                factor = jnp.where(
                    left_head,
                    inverse[head : head + BOTH, j : j + 1],
                    inverse[head + BOTH : head + 2 * BOTH, j : j + 1],
                )
                outs.append((out * factor).astype(BF16))
            out = jnp.concatenate(outs, 1)
            om_ref[g * PACK + j] = out[:STRIP]
            oo_ref[g * PACK + j] = out[STRIP:]

    by_pack(first, cols, body)


def column_part(info, mine, other, recv_mine, recv_other, weights, first, cols):
    width = mine.shape[-1]
    heads = width // HEAD_DIM
    shape = jax.ShapeDtypeStruct((cols, STRIP, width), BF16)
    return call(
        functools.partial(column_kernel, heads=heads, first=first, cols=cols),
        info,
        [mine, other, recv_mine, recv_other, weights],
        [shape, shape],
        [pltpu.VMEM((2, cols, heads * BOTH), F32)],
        name="column_attention",
    )


def mix_kernel(info, *refs, first, cols, parts):
    row_refs, near_ref, far_ref = refs[:parts], refs[parts], refs[parts + 1]
    out_ref, out_buf, out_sem = refs[-3:]
    copies = []
    for o, ref in enumerate((near_ref, far_ref)):
        span = column_span(info, o == 1, first, cols)
        column = jnp.swapaxes(ref[...], 0, 1).astype(F32)
        at = 0
        for row_ref in row_refs:
            rows = slice(at, at + row_ref.shape[0])
            out_buf[o, rows] = (0.5 * (row_ref[:, span, :] + column[rows])).astype(BF16)
            at += row_ref.shape[0]
        copy = pltpu.make_async_copy(out_buf.at[o], out_ref.at[:, span, :], out_sem.at[o])
        copy.start()
        copies.append(copy)
    for copy in copies:
        copy.wait()


def mix(info, row_context, near, far, done, first):
    cols, _, width = near.shape
    parts = len(row_context)
    operands = list(row_context) + [near, far]
    in_specs = [ON_CHIP] * len(operands)
    aliases = {}
    if done is not None:
        operands.append(done)
        in_specs.append(ANYWHERE)
        aliases = {len(operands): 0}
    return call(
        functools.partial(mix_kernel, first=first, cols=cols, parts=parts),
        info,
        operands,
        jax.ShapeDtypeStruct((STRIP, COLS, width), BF16),
        [pltpu.VMEM((2, STRIP, cols, width), BF16), pltpu.SemaphoreType.DMA((2,))],
        in_specs=in_specs,
        out_specs=ANYWHERE,
        aliases=aliases,
        name="mix",
    )


CORE_SWAP = [(0, 1), (1, 0), (2, 3), (3, 2)]
SAME_CORE = [(0, 2), (1, 3), (2, 0), (3, 1)]
OTHER_CORE = [(0, 3), (1, 2), (2, 1), (3, 0)]
DOWN_SAME = [(0, 2), (1, 3)]
UP_SAME = [(2, 0), (3, 1)]
NEXT_STRIP = [(0, 1), (1, 2), (2, 3)]


def send(block, route):
    return pltpu.with_memory_space_constraint(lax.ppermute(block, "seq", route), pltpu.VMEM)


def in_hbm(array):
    return pltpu.with_memory_space_constraint(array, pltpu.HBM)


def after(value, *earlier):
    return lax.optimization_barrier((value,) + earlier)[0]


def two_chips(patches, w_qkv):
    width = w_qkv.shape[2]
    chunks = ((0, 64), (64, 64))
    seq = lax.axis_index("seq")
    info = jnp.stack([seq % 2, seq // 2, seq]).astype(jnp.int32)
    x = patches.reshape(STRIP, COLS, D)
    w = jnp.transpose(w_qkv, (1, 0, 2))

    first = project(info, in_hbm(x), in_hbm(w))
    recv_mine = send(first[4], SAME_CORE)
    natural, mine, other, last = project_rest(info, first[6], w, first[:4])
    other = send(other, CORE_SWAP)
    halo = send(last, NEXT_STRIP)
    recv_other = send(after(first[5], last), OTHER_CORE)
    info = after(info, recv_mine, halo)
    rows_low = row_part(info, None, natural, 8, 8)
    info = after(info, rows_low)
    rows_top = row_part(info, halo, natural, 0, 8)
    info = after(info, rows_top)
    top = maxima(info, mine, other)
    below = send(top, UP_SAME)
    info = after(info, top)
    far = []
    for at, cols in chunks:
        weights = cross_weights(info, recv_mine, recv_other, mine, other, below, at, cols)
        info = after(info, weights)
        far.append(send(weights, DOWN_SAME))
    out = None
    for (at, cols), weights in zip(chunks, far):
        near, remote = column_part(info, mine, other, recv_mine, recv_other, weights, at, cols)
        remote = send(remote, CORE_SWAP)
        out = mix(info, (rows_top, rows_low), near, remote, out, at)
        info = after(info, out)
    return out.reshape(STRIP * COLS, width)


def local(patches, w_qkv):
    shape_fits = patches.shape[0] == STRIP * COLS and w_qkv.shape[2] == 4 * HEAD_DIM
    if lax.axis_size("seq") == 4 and shape_fits:
        return two_chips(patches, w_qkv)
    return general(patches, w_qkv)


def solution(mesh):
    placed = (P(("groups", "seq"), None), P(None, None, "head"))
    return jax.shard_map(
        local, mesh=mesh, in_specs=placed, out_specs=P(("groups", "seq"), "head"), check_vma=False
    )
```

```python
import functools
import math

import jax
import jax.numpy as jnp
from jax import lax
from jax.experimental import pallas as pl
from jax.experimental.pallas import tpu as pltpu
from jax.sharding import PartitionSpec as P

D = 1024
HEAD_DIM = 64
COLS = 256
NEG_BIG = -1e30

STRIP = 16
BOTH = 2 * STRIP
PACK = 4

F32 = jnp.float32
BF16 = jnp.bfloat16


def shifted(block, axis, distance):
    devices = range(lax.axis_size(axis))
    route = [(i - distance, i) for i in devices if i - distance in devices]
    return lax.ppermute(block, axis, route)


def row_attention(queries, key_rows, value_rows, prev_keys, prev_values, first_row):
    row_count = queries.shape[1]
    scale = 1.0 / math.sqrt(HEAD_DIM)
    earlier_keys = jnp.concatenate([prev_keys[:, None], key_rows[:, :-1]], 1)
    earlier_values = jnp.concatenate([prev_values[:, None], value_rows[:, :-1]], 1)
    score_prev = (
        jnp.einsum("hrce,hrje->hrcj", queries, earlier_keys, preferred_element_type=jnp.float32)
        * scale
    )
    score_own = (
        jnp.einsum("hrce,hrje->hrcj", queries, key_rows, preferred_element_type=jnp.float32) * scale
    )
    column = lax.broadcasted_iota(jnp.int32, (1, 1, COLS, COLS), 2)
    slot = lax.broadcasted_iota(jnp.int32, (1, 1, COLS, COLS), 3)
    row_index = lax.broadcasted_iota(jnp.int32, (1, row_count, 1, 1), 1) + first_row
    allowed_prev = (slot > column) & (row_index > 0)
    allowed_own = slot <= column
    score_prev = jnp.where(allowed_prev, score_prev, NEG_BIG)
    score_own = jnp.where(allowed_own, score_own, NEG_BIG)
    highest = jnp.maximum(
        jnp.max(score_prev, axis=-1, keepdims=True), jnp.max(score_own, axis=-1, keepdims=True)
    )
    terms_prev = jnp.where(allowed_prev, jnp.exp(score_prev - highest), 0.0)
    terms_own = jnp.where(allowed_own, jnp.exp(score_own - highest), 0.0)
    totals = jnp.sum(terms_prev, axis=-1, keepdims=True) + jnp.sum(
        terms_own, axis=-1, keepdims=True
    )
    context = jnp.einsum(
        "hrcj,hrje->hrce",
        terms_prev.astype(jnp.bfloat16),
        earlier_values,
        preferred_element_type=jnp.float32,
    )
    context = context + jnp.einsum(
        "hrcj,hrje->hrce",
        terms_own.astype(jnp.bfloat16),
        value_rows,
        preferred_element_type=jnp.float32,
    )
    return context / totals


def column_attention(queries, key_rows, value_rows):
    row_count = queries.shape[1]
    scores = jnp.einsum(
        "hrce,hsce->hcrs", queries, key_rows, preferred_element_type=jnp.float32
    ) * (1.0 / math.sqrt(HEAD_DIM))
    later = lax.broadcasted_iota(jnp.int32, (1, 1, row_count, row_count), 2)
    earlier = lax.broadcasted_iota(jnp.int32, (1, 1, row_count, row_count), 3)
    allowed = earlier <= later
    scores = jnp.where(allowed, scores, NEG_BIG)
    highest = jnp.max(scores, axis=-1, keepdims=True)
    terms = jnp.where(allowed, jnp.exp(scores - highest), 0.0)
    totals = jnp.sum(terms, axis=-1, keepdims=True)
    context = jnp.einsum(
        "hcrs,hsce->hcre",
        terms.astype(jnp.bfloat16),
        value_rows,
        preferred_element_type=jnp.float32,
    )
    return jnp.transpose((context / totals).astype(jnp.bfloat16), (0, 2, 1, 3))


def general(patches, w_qkv):
    local_width = w_qkv.shape[2]
    head_count = local_width // HEAD_DIM
    row_count = patches.shape[0] // COLS
    weights_heads = w_qkv.reshape(D, 3, head_count, HEAD_DIM)
    projected = jnp.einsum(
        "td,dkhe->khte", patches, weights_heads, preferred_element_type=jnp.float32
    ).astype(jnp.bfloat16)
    prev_inputs = shifted(patches[-COLS:], "seq", 1)
    prev_pair = jnp.einsum(
        "td,dkhe->khte", prev_inputs, weights_heads[:, 1:], preferred_element_type=jnp.float32
    ).astype(jnp.bfloat16)
    first_row = lax.axis_index("seq") * row_count
    stacked = projected.reshape(3, head_count, row_count, COLS, HEAD_DIM)
    row_context = row_attention(
        stacked[0], stacked[1], stacked[2], prev_pair[0], prev_pair[1], first_row
    )
    column_pack = lax.all_to_all(stacked, "seq", split_axis=3, concat_axis=2, tiled=True)
    column_context = column_attention(column_pack[0], column_pack[1], column_pack[2])
    returned = lax.all_to_all(column_context, "seq", split_axis=1, concat_axis=2, tiled=True)
    mixed = (0.5 * (row_context + returned.astype(jnp.float32))).astype(jnp.bfloat16)
    return jnp.transpose(mixed, (1, 2, 0, 3)).reshape(row_count * COLS, local_width)


def iota(shape, axis):
    return lax.broadcasted_iota(jnp.int32, shape, axis)


def dot(left, right):
    return jnp.dot(left, right, preferred_element_type=F32)


def dot_t(left, right):
    return lax.dot_general(left, right, (((1,), (1,)), ((), ())), preferred_element_type=F32)


SLICES = 3
HALF = COLS // 2
LONG = 4 * 10**10
SPLIT = HALF // 2
ANYWHERE = pl.BlockSpec(memory_space=pl.ANY)
ON_CHIP = pl.BlockSpec(memory_space=pltpu.VMEM)


def call(kernel, info, operands, out_shape, scratch=(), **more):
    options = dict(
        in_specs=[ON_CHIP] * len(operands),
        out_specs=jax.tree.map(lambda _: ON_CHIP, out_shape),
    )
    aliases = more.pop("aliases", {})
    name = more.pop("name")
    flops = more.pop("flops", 1)
    options.update(more)
    return pl.pallas_call(
        kernel,
        out_shape=out_shape,
        grid_spec=pltpu.PrefetchScalarGridSpec(
            num_scalar_prefetch=1,
            grid=options.pop("grid", ()),
            scratch_shapes=list(scratch),
            **options,
        ),
        input_output_aliases=aliases,
        compiler_params=pltpu.CompilerParams(vmem_limit_bytes=28 << 20),
        cost_estimate=pl.CostEstimate(flops=flops, bytes_accessed=1, transcendentals=0),
        name=name,
    )(info, *operands)


def column_span(info, other, first, cols):
    half = 1 - info[0] if other else info[0]
    return pl.ds(pl.multiple_of(half * HALF + first, 16), cols)


def sent_slot(info):
    return jnp.where(info[1] == 0, 2, 0)


def projected(x, w, natural_ref, last_ref, turned_refs, slot, columns):
    _, block, depth = x.shape
    part = STRIP // 2
    parts = [
        dot(x[r : r + part].reshape(part * block, depth), w).astype(BF16) for r in (0, part)
    ]
    value = jnp.concatenate(parts, 0).reshape(STRIP, block, w.shape[1])
    natural_ref[slot, :, columns, :] = value

    @pl.when(slot > 0)
    def _():
        last_ref[slot - 1, columns, :] = value[STRIP - 1]

    turned = jnp.swapaxes(value, 0, 1)
    for ref in turned_refs:
        ref[...] = turned


def first_kernel(info, x_ref, w_ref, *refs, block):
    natural_ref, mine_ref, other_ref, last_ref, send_mine_ref = refs[:5]
    send_others, x_out, w_buf, x_sem, w_sem = refs[5:7], refs[7], *refs[8:]
    slot = sent_slot(info)
    w_copy = pltpu.make_async_copy(w_ref.at[slot], w_buf, w_sem)
    w_copy.start()
    pieces = []
    for other in (False, True):
        for first in range(0, HALF, block):
            columns = column_span(info, other, first, block)
            copy = pltpu.make_async_copy(
                x_ref.at[:, columns, :], x_out.at[:, columns, :], x_sem.at[len(pieces)]
            )
            copy.start()
            pieces.append((copy, other, first, columns))
    w_copy.wait()
    w = w_buf[...]
    for copy, other, first, columns in pieces:
        copy.wait()
        triple_ref = other_ref if other else mine_ref
        if other:
            send_ref = send_others[first // SPLIT].at[pl.ds(first % SPLIT, block)]
        else:
            send_ref = send_mine_ref.at[pl.ds(first, block)]
        projected(
            x_out[:, columns, :],
            w,
            natural_ref,
            last_ref,
            (triple_ref.at[slot, pl.ds(first, block)], send_ref),
            slot,
            columns,
        )


def rest_kernel(info, x_ref, w_ref, *refs, block):
    natural_ref, mine_ref, other_ref, last_ref = refs[-4:]
    for slot in (2 - sent_slot(info), 1):
        w = w_ref[slot]
        for other, triple_ref in ((False, mine_ref), (True, other_ref)):
            for first in range(0, HALF, block):
                columns = column_span(info, other, first, block)
                projected(
                    x_ref[:, columns, :],
                    w,
                    natural_ref,
                    last_ref,
                    (triple_ref.at[slot, pl.ds(first, block)],),
                    slot,
                    columns,
                )


def project(info, x, w, block=64):
    width = w.shape[2]
    natural = jax.ShapeDtypeStruct((3, STRIP, COLS, width), BF16)
    triple = jax.ShapeDtypeStruct((3, HALF, STRIP, width), BF16)
    last = jax.ShapeDtypeStruct((2, COLS, width), BF16)
    sends = [jax.ShapeDtypeStruct((n, STRIP, width), BF16) for n in (HALF, SPLIT, HALF - SPLIT)]
    return call(
        functools.partial(first_kernel, block=block),
        info,
        [x, w],
        [natural, triple, triple, last] + sends + [jax.ShapeDtypeStruct(x.shape, BF16)],
        [
            pltpu.VMEM(w.shape[1:], BF16),
            pltpu.SemaphoreType.DMA((COLS // block,)),
            pltpu.SemaphoreType.DMA,
        ],
        in_specs=[ANYWHERE] * 2,
        name="project_sent",
    )


def project_rest(info, x, w, kept, block=64):
    return call(
        functools.partial(rest_kernel, block=block),
        info,
        [x, w] + list(kept),
        [jax.ShapeDtypeStruct(array.shape, BF16) for array in kept],
        aliases={3 + n: n for n in range(len(kept))},
        name="project_rest",
    )


def heads_of(shape, axis):
    return iota(shape, axis) // HEAD_DIM


def head_rows(rows_per_head, width):
    shape = (rows_per_head * (width // HEAD_DIM), width)
    own = iota(shape, 0) // rows_per_head == iota(shape, 1) // HEAD_DIM
    return jnp.where(own, 1.0 / math.sqrt(HEAD_DIM), 0.0).astype(BF16)


def row_kernel(info, *refs, width, top, rows):
    before_k_ref, before_v_ref, q_ref, k_ref, v_ref, out_ref, prev_k, prev_v = refs
    step = pl.program_id(0)
    heads = width // HEAD_DIM

    @pl.when(step == 0)
    def _():
        prev_k[...] = before_k_ref[0] if top else before_k_ref[0, 0]
        prev_v[...] = before_v_ref[0] if top else before_v_ref[0, 0]

    own = iota((COLS, COLS), 1) <= iota((COLS, COLS), 0)
    lane_head = heads_of((COLS, width), 1)
    scale = 1.0 / math.sqrt(HEAD_DIM)
    spread = [jnp.where(lane_head == h, scale, 0.0).astype(BF16) for h in range(heads)]
    earlier_k, earlier_v = prev_k[...], prev_v[...]
    for r in range(rows):
        q, k, v = q_ref[0, r], k_ref[0, r], v_ref[0, r]
        result = None
        for h in range(heads):
            masked = q * spread[h]
            scores_prev = dot_t(masked, earlier_k)
            if top and r == 0:
                first = (step == 0) & (info[2] == 0)
                scores_prev = scores_prev + jnp.where(first, NEG_BIG, 0.0)
            scores = jnp.where(own, dot_t(masked, k), scores_prev)
            terms = jnp.exp(scores - jnp.max(scores, axis=1, keepdims=True))
            inverse = 1.0 / jnp.sum(terms, axis=1, keepdims=True)
            context = dot(jnp.where(own, terms, 0.0).astype(BF16), v)
            context = context + dot(jnp.where(own, 0.0, terms).astype(BF16), earlier_v)
            context = context * inverse
            result = context if h == 0 else jnp.where(lane_head == h, context, result)
        out_ref[r] = result
        earlier_k, earlier_v = k, v
    prev_k[...] = earlier_k
    prev_v[...] = earlier_v


def row_part(info, halo, natural, first_row, row_count, rows=4):
    width = natural.shape[3]
    top = first_row == 0
    block = (1, rows, COLS, width)

    def spec(slot):
        return pl.BlockSpec(block, lambda r, info: (slot, first_row // rows + r, 0, 0))

    def before_spec(slot):
        if top:
            return pl.BlockSpec((1, COLS, width), lambda r, info: (slot - 1, 0, 0))
        return pl.BlockSpec((1, 1, COLS, width), lambda r, info: (slot, first_row - 1, 0, 0))

    return call(
        functools.partial(row_kernel, width=width, top=top, rows=rows),
        info,
        [halo if top else natural] * 2 + [natural] * 3,
        jax.ShapeDtypeStruct((row_count, COLS, width), F32),
        [pltpu.VMEM((COLS, width), BF16)] * 2,
        grid=(row_count // rows,),
        in_specs=[before_spec(1), before_spec(2)] + [spec(slot) for slot in range(3)],
        out_specs=pl.BlockSpec((rows, COLS, width), lambda r, info: (r, 0, 0)),
        flops=LONG,
        name="row_attention",
    )


def column_of(mine, other, j):
    return jnp.concatenate([mine[j], other[j]], 0)


def scores_of(keys, queries, spread, heads):
    return dot_t(keys, jnp.concatenate([queries] * heads, 0) * spread)


def later_key(core, heads):
    shape = (BOTH, heads * BOTH)
    key_row = (iota(shape, 0) + STRIP * core) & (BOTH - 1)
    query_row = (iota(shape, 1) + STRIP * core) & (BOTH - 1)
    return key_row > query_row


def by_pack(first, count, body):
    def run(g, carry):
        body(g, pl.ds(first + g * PACK, PACK))
        return carry

    lax.fori_loop(0, count // PACK, run, 0, unroll=4)


def maxima_kernel(info, mine_ref, other_ref, out_ref, *, heads):
    hidden = later_key(info[0], heads)
    spread = head_rows(BOTH, heads * HEAD_DIM)

    def body(g, part):
        qm, qo = mine_ref[0, part], other_ref[0, part]
        km, ko = mine_ref[1, part], other_ref[1, part]
        tops = []
        for j in range(PACK):
            scores = scores_of(column_of(km, ko, j), column_of(qm, qo, j), spread, heads)
            tops.append(jnp.max(jnp.where(hidden, NEG_BIG, scores), axis=0, keepdims=True))
        out_ref[part] = jnp.concatenate(tops, 0)

    @pl.when(info[1] == 1)
    def _():
        by_pack(0, mine_ref.shape[1], body)


def maxima(info, mine, other):
    heads = mine.shape[-1] // HEAD_DIM
    return call(
        functools.partial(maxima_kernel, heads=heads),
        info,
        [mine, other],
        jax.ShapeDtypeStruct((mine.shape[1], heads * BOTH), F32),
        name="maxima",
    )


def weights_kernel(
    info, qm_ref, qo_ref, mine_ref, other_ref, top_ref, w_ref, stats, *, heads, first, cols, base
):
    spread = head_rows(BOTH, heads * HEAD_DIM)

    def body(g, part):
        qm, qo = qm_ref[part], qo_ref[pl.ds(first - base + g * PACK, PACK)]
        km, ko = mine_ref[1, part], other_ref[1, part]
        below = top_ref[part]
        tops, totals, turned = [], [], []
        for j in range(PACK):
            scores = scores_of(column_of(km, ko, j), column_of(qm, qo, j), spread, heads)
            top = jnp.maximum(jnp.max(scores, axis=0, keepdims=True), below[j : j + 1])
            terms = jnp.exp(scores - top)
            tops.append(top)
            totals.append(jnp.sum(terms, axis=0, keepdims=True))
            turned.append(terms)
        w_ref[pl.ds(g * heads * BOTH, heads * BOTH)] = jnp.concatenate(turned, 0).T.astype(BF16)
        stats[0, pl.ds(g * PACK, PACK)] = jnp.concatenate(tops, 0)
        stats[1, pl.ds(g * PACK, PACK)] = jnp.concatenate(totals, 0)

    @pl.when(info[1] == 0)
    def _():
        by_pack(first, cols, body)
        rest = stats[...].reshape(2 * cols, heads * BOTH)
        at = cols // PACK * heads * BOTH
        for n in range(SLICES):
            part = rest.astype(BF16)
            w_ref[at + n * 2 * cols : at + (n + 1) * 2 * cols] = part
            rest = rest - part.astype(F32)


def cross_weights(info, recv_mine, recv_other, mine, other, top, first, cols, base):
    heads = mine.shape[-1] // HEAD_DIM
    rows = heads * BOTH
    return call(
        functools.partial(weights_kernel, heads=heads, first=first, cols=cols, base=base),
        info,
        [recv_mine, recv_other, mine, other, top],
        jax.ShapeDtypeStruct((cols // PACK * rows + SLICES * 2 * cols, PACK * BOTH), BF16),
        [pltpu.VMEM((2, cols, rows), F32)],
        name="cross_weights",
    )


def column_kernel(
    info, mine_ref, other_ref, vm_ref, vo_ref, w_ref, om_ref, oo_ref, stats, *, heads, first, cols, base
):
    hidden = later_key(info[0], heads)
    width = heads * HEAD_DIM
    rows = heads * BOTH
    spread = head_rows(BOTH, width)
    lower = info[1] == 1
    pair = 2 * BOTH
    keys = PACK * BOTH
    key_column = (iota((1, 2 * keys), 1) & (keys - 1)) // BOTH
    picks = [jnp.where(key_column == j, 1.0, 0.0).astype(BF16) for j in range(PACK)]
    left_head = iota((BOTH, 2 * HEAD_DIM), 1) < HEAD_DIM
    at = cols // PACK * rows
    whole = w_ref[at : at + 2 * cols].astype(F32)
    for n in range(1, SLICES):
        whole = whole + w_ref[at + n * 2 * cols : at + (n + 1) * 2 * cols].astype(F32)
    stats[...] = whole.reshape(stats.shape)

    def body(g, part):
        local = pl.ds(g * PACK, PACK)
        qm, qo = mine_ref[0, part], other_ref[0, part]
        km, ko = mine_ref[1, part], other_ref[1, part]
        above, far_totals = stats[0, local], stats[1, local]
        totals, turned = [], []
        for j in range(PACK):
            scores = scores_of(column_of(km, ko, j), column_of(qm, qo, j), spread, heads)
            scores = jnp.where(hidden, NEG_BIG, scores)
            top = jnp.max(scores, axis=0, keepdims=True)
            top = jnp.where(lower, above[j : j + 1], top)
            terms = jnp.exp(scores - top)
            totals.append(jnp.sum(terms, axis=0, keepdims=True))
            turned.append(terms)
        inverse = 1.0 / (jnp.concatenate(totals, 0) + far_totals)
        inverse = jnp.concatenate([inverse, inverse], 0).T
        near = jnp.concatenate(turned, 0).T.astype(BF16)
        weights = jnp.concatenate([near, w_ref[pl.ds(g * rows, rows)]], 1)
        near_v = [column_of(mine_ref[2, part], other_ref[2, part], j) for j in range(PACK)]
        vm, vo = vm_ref[part], vo_ref[pl.ds(first - base + g * PACK, PACK)]
        far_v = [column_of(vm, vo, j) for j in range(PACK)]
        values = jnp.concatenate(near_v + far_v, 0)
        left = jnp.concatenate([weights * picks[j] for j in range(PACK)], 0)
        context = dot(left, values)
        for j in range(PACK):
            outs = []
            for t in range(heads // 2):
                lanes = slice(t * 2 * HEAD_DIM, (t + 1) * 2 * HEAD_DIM)
                at = j * rows + t * pair
                head = t * pair
                out = jnp.where(
                    left_head,
                    context[at : at + BOTH, lanes],
                    context[at + BOTH : at + 2 * BOTH, lanes],
                )
                factor = jnp.where(
                    left_head,
                    inverse[head : head + BOTH, j : j + 1],
                    inverse[head + BOTH : head + 2 * BOTH, j : j + 1],
                )
                outs.append((out * factor).astype(BF16))
            out = jnp.concatenate(outs, 1)
            om_ref[g * PACK + j] = out[:STRIP]
            oo_ref[g * PACK + j] = out[STRIP:]

    by_pack(first, cols, body)


def column_part(info, mine, other, recv_mine, recv_other, weights, first, cols, base, flops):
    width = mine.shape[-1]
    heads = width // HEAD_DIM
    shape = jax.ShapeDtypeStruct((cols, STRIP, width), BF16)
    return call(
        functools.partial(column_kernel, heads=heads, first=first, cols=cols, base=base),
        info,
        [mine, other, recv_mine, recv_other, weights],
        [shape, shape],
        [pltpu.VMEM((2, cols, heads * BOTH), F32)],
        flops=flops,
        name="column_attention",
    )


def mix_kernel(info, *refs, first, cols, parts):
    row_refs, near_ref, far_ref = refs[:parts], refs[parts], refs[parts + 1]
    out_ref, out_buf, out_sem = refs[-3:]
    copies = []
    for o, ref in enumerate((near_ref, far_ref)):
        span = column_span(info, o == 1, first, cols)
        column = jnp.swapaxes(ref[...], 0, 1).astype(F32)
        at = 0
        for row_ref in row_refs:
            rows = slice(at, at + row_ref.shape[0])
            out_buf[o, rows] = (0.5 * (row_ref[:, span, :] + column[rows])).astype(BF16)
            at += row_ref.shape[0]
        copy = pltpu.make_async_copy(out_buf.at[o], out_ref.at[:, span, :], out_sem.at[o])
        copy.start()
        copies.append(copy)
    for copy in copies:
        copy.wait()


def mix(info, row_context, near, far, done, first):
    cols, _, width = near.shape
    parts = len(row_context)
    operands = list(row_context) + [near, far]
    in_specs = [ON_CHIP] * len(operands)
    aliases = {}
    if done is not None:
        operands.append(done)
        in_specs.append(ANYWHERE)
        aliases = {len(operands): 0}
    return call(
        functools.partial(mix_kernel, first=first, cols=cols, parts=parts),
        info,
        operands,
        jax.ShapeDtypeStruct((STRIP, COLS, width), BF16),
        [pltpu.VMEM((2, STRIP, cols, width), BF16), pltpu.SemaphoreType.DMA((2,))],
        in_specs=in_specs,
        out_specs=ANYWHERE,
        aliases=aliases,
        name="mix",
    )


CORE_SWAP = [(0, 1), (1, 0), (2, 3), (3, 2)]
SAME_CORE = [(0, 2), (1, 3), (2, 0), (3, 1)]
OTHER_CORE = [(0, 3), (1, 2), (2, 1), (3, 0)]
DOWN_SAME = [(0, 2), (1, 3)]
UP_SAME = [(2, 0), (3, 1)]
NEXT_STRIP = [(0, 1), (1, 2), (2, 3)]


def send(block, route):
    return pltpu.with_memory_space_constraint(lax.ppermute(block, "seq", route), pltpu.VMEM)


def in_hbm(array):
    return pltpu.with_memory_space_constraint(array, pltpu.HBM)


def after(value, *earlier):
    return lax.optimization_barrier((value,) + earlier)[0]


def two_chips(patches, w_qkv):
    width = w_qkv.shape[2]
    chunks = ((0, 64), (64, 32), (96, 32))
    seq = lax.axis_index("seq")
    info = jnp.stack([seq % 2, seq // 2, seq]).astype(jnp.int32)
    x = patches.reshape(STRIP, COLS, D)
    w = jnp.transpose(w_qkv, (1, 0, 2))

    first = project(info, in_hbm(x), in_hbm(w))
    recv_mine = send(first[4], SAME_CORE)
    natural, mine, other, last = project_rest(info, first[7], w, first[:4])
    other = send(other, CORE_SWAP)
    halo = send(last, NEXT_STRIP)
    recv_others = [send(after(first[5], last), OTHER_CORE)]
    info = after(info, recv_mine, halo)
    rows_low = row_part(info, None, natural, 8, 8)
    info = after(info, rows_low)
    top = maxima(info, mine, other)
    below = send(top, UP_SAME)
    recv_others.append(send(after(first[6], top), OTHER_CORE))
    info = after(info, top)
    far = []
    for n, (at, cols) in enumerate(chunks):
        part = at // SPLIT
        weights = cross_weights(
            info, recv_mine, recv_others[part], mine, other, below, at, cols, part * SPLIT
        )
        info = after(info, weights)
        far.append(send(weights, DOWN_SAME))
        if n == 0:
            rows_top = row_part(info, halo, natural, 0, 8)
            info = after(info, rows_top)
    row_context = (rows_top, rows_low)
    pending = []
    out = None
    for n, ((at, cols), weights) in enumerate(zip(chunks, far)):
        part = at // SPLIT
        near, remote = column_part(
            info,
            mine,
            other,
            recv_mine,
            recv_others[part],
            weights,
            at,
            cols,
            part * SPLIT,
            LONG if n > 0 else 1,
        )
        info = after(info, near)
        pending.append((near, send(remote, CORE_SWAP), at))
        if n > 0:
            near, remote, at = pending.pop(0)
            out = mix(info, row_context, near, remote, out, at)
            info = after(info, out)
    near, remote, at = pending.pop(0)
    out = mix(info, row_context, near, remote, out, at)
    return out.reshape(STRIP * COLS, width)


def local(patches, w_qkv):
    shape_fits = patches.shape[0] == STRIP * COLS and w_qkv.shape[2] == 4 * HEAD_DIM
    if lax.axis_size("seq") == 4 and shape_fits:
        return two_chips(patches, w_qkv)
    return general(patches, w_qkv)


def solution(mesh):
    placed = (P(("groups", "seq"), None), P(None, None, "head"))
    return jax.shard_map(
        local, mesh=mesh, in_specs=placed, out_specs=P(("groups", "seq"), "head"), check_vma=False
    )
```

```python
import functools
import math

import jax
import jax.numpy as jnp
from jax import lax
from jax.experimental import pallas as pl
from jax.experimental.pallas import tpu as pltpu
from jax.sharding import PartitionSpec as P

D = 1024
HEAD_DIM = 64
COLS = 256
NEG_BIG = -1e30

STRIP = 16
BOTH = 2 * STRIP
PACK = 4

F32 = jnp.float32
BF16 = jnp.bfloat16


def shifted(block, axis, distance):
    devices = range(lax.axis_size(axis))
    route = [(i - distance, i) for i in devices if i - distance in devices]
    return lax.ppermute(block, axis, route)


def row_attention(queries, key_rows, value_rows, prev_keys, prev_values, first_row):
    row_count = queries.shape[1]
    scale = 1.0 / math.sqrt(HEAD_DIM)
    earlier_keys = jnp.concatenate([prev_keys[:, None], key_rows[:, :-1]], 1)
    earlier_values = jnp.concatenate([prev_values[:, None], value_rows[:, :-1]], 1)
    score_prev = (
        jnp.einsum("hrce,hrje->hrcj", queries, earlier_keys, preferred_element_type=jnp.float32)
        * scale
    )
    score_own = (
        jnp.einsum("hrce,hrje->hrcj", queries, key_rows, preferred_element_type=jnp.float32) * scale
    )
    column = lax.broadcasted_iota(jnp.int32, (1, 1, COLS, COLS), 2)
    slot = lax.broadcasted_iota(jnp.int32, (1, 1, COLS, COLS), 3)
    row_index = lax.broadcasted_iota(jnp.int32, (1, row_count, 1, 1), 1) + first_row
    allowed_prev = (slot > column) & (row_index > 0)
    allowed_own = slot <= column
    score_prev = jnp.where(allowed_prev, score_prev, NEG_BIG)
    score_own = jnp.where(allowed_own, score_own, NEG_BIG)
    highest = jnp.maximum(
        jnp.max(score_prev, axis=-1, keepdims=True), jnp.max(score_own, axis=-1, keepdims=True)
    )
    terms_prev = jnp.where(allowed_prev, jnp.exp(score_prev - highest), 0.0)
    terms_own = jnp.where(allowed_own, jnp.exp(score_own - highest), 0.0)
    totals = jnp.sum(terms_prev, axis=-1, keepdims=True) + jnp.sum(
        terms_own, axis=-1, keepdims=True
    )
    context = jnp.einsum(
        "hrcj,hrje->hrce",
        terms_prev.astype(jnp.bfloat16),
        earlier_values,
        preferred_element_type=jnp.float32,
    )
    context = context + jnp.einsum(
        "hrcj,hrje->hrce",
        terms_own.astype(jnp.bfloat16),
        value_rows,
        preferred_element_type=jnp.float32,
    )
    return context / totals


def column_attention(queries, key_rows, value_rows):
    row_count = queries.shape[1]
    scores = jnp.einsum(
        "hrce,hsce->hcrs", queries, key_rows, preferred_element_type=jnp.float32
    ) * (1.0 / math.sqrt(HEAD_DIM))
    later = lax.broadcasted_iota(jnp.int32, (1, 1, row_count, row_count), 2)
    earlier = lax.broadcasted_iota(jnp.int32, (1, 1, row_count, row_count), 3)
    allowed = earlier <= later
    scores = jnp.where(allowed, scores, NEG_BIG)
    highest = jnp.max(scores, axis=-1, keepdims=True)
    terms = jnp.where(allowed, jnp.exp(scores - highest), 0.0)
    totals = jnp.sum(terms, axis=-1, keepdims=True)
    context = jnp.einsum(
        "hcrs,hsce->hcre",
        terms.astype(jnp.bfloat16),
        value_rows,
        preferred_element_type=jnp.float32,
    )
    return jnp.transpose((context / totals).astype(jnp.bfloat16), (0, 2, 1, 3))


def general(patches, w_qkv):
    local_width = w_qkv.shape[2]
    head_count = local_width // HEAD_DIM
    row_count = patches.shape[0] // COLS
    weights_heads = w_qkv.reshape(D, 3, head_count, HEAD_DIM)
    projected = jnp.einsum(
        "td,dkhe->khte", patches, weights_heads, preferred_element_type=jnp.float32
    ).astype(jnp.bfloat16)
    prev_inputs = shifted(patches[-COLS:], "seq", 1)
    prev_pair = jnp.einsum(
        "td,dkhe->khte", prev_inputs, weights_heads[:, 1:], preferred_element_type=jnp.float32
    ).astype(jnp.bfloat16)
    first_row = lax.axis_index("seq") * row_count
    stacked = projected.reshape(3, head_count, row_count, COLS, HEAD_DIM)
    row_context = row_attention(
        stacked[0], stacked[1], stacked[2], prev_pair[0], prev_pair[1], first_row
    )
    column_pack = lax.all_to_all(stacked, "seq", split_axis=3, concat_axis=2, tiled=True)
    column_context = column_attention(column_pack[0], column_pack[1], column_pack[2])
    returned = lax.all_to_all(column_context, "seq", split_axis=1, concat_axis=2, tiled=True)
    mixed = (0.5 * (row_context + returned.astype(jnp.float32))).astype(jnp.bfloat16)
    return jnp.transpose(mixed, (1, 2, 0, 3)).reshape(row_count * COLS, local_width)


def iota(shape, axis):
    return lax.broadcasted_iota(jnp.int32, shape, axis)


def dot(left, right):
    return jnp.dot(left, right, preferred_element_type=F32)


def dot_t(left, right):
    return lax.dot_general(left, right, (((1,), (1,)), ((), ())), preferred_element_type=F32)


SLICES = 3
HALF = COLS // 2
LONG = 4 * 10**10
SPLIT = HALF // 2
ANYWHERE = pl.BlockSpec(memory_space=pl.ANY)
ON_CHIP = pl.BlockSpec(memory_space=pltpu.VMEM)


def call(kernel, info, operands, out_shape, scratch=(), **more):
    options = dict(
        in_specs=[ON_CHIP] * len(operands),
        out_specs=jax.tree.map(lambda _: ON_CHIP, out_shape),
    )
    aliases = more.pop("aliases", {})
    name = more.pop("name")
    flops = more.pop("flops", 1)
    options.update(more)
    return pl.pallas_call(
        kernel,
        out_shape=out_shape,
        grid_spec=pltpu.PrefetchScalarGridSpec(
            num_scalar_prefetch=1,
            grid=options.pop("grid", ()),
            scratch_shapes=list(scratch),
            **options,
        ),
        input_output_aliases=aliases,
        compiler_params=pltpu.CompilerParams(vmem_limit_bytes=20 << 20),
        cost_estimate=pl.CostEstimate(flops=flops, bytes_accessed=1, transcendentals=0),
        name=name,
    )(info, *operands)


def column_span(info, other, first, cols):
    half = 1 - info[0] if other else info[0]
    return pl.ds(pl.multiple_of(half * HALF + first, 16), cols)


def sent_slot(info):
    return jnp.where(info[1] == 0, 2, 0)


def projected(x, w, natural_ref, last_ref, turned_refs, slot, columns):
    _, block, depth = x.shape
    part = STRIP // 2
    parts = [
        dot(x[r : r + part].reshape(part * block, depth), w).astype(BF16) for r in (0, part)
    ]
    value = jnp.concatenate(parts, 0).reshape(STRIP, block, w.shape[1])
    natural_ref[slot, :, columns, :] = value

    @pl.when(slot > 0)
    def _():
        last_ref[slot - 1, columns, :] = value[STRIP - 1]

    turned = jnp.swapaxes(value, 0, 1)
    for ref in turned_refs:
        ref[...] = turned


def sent_kernel(info, x_ref, w_ref, *refs, other, sends, block):
    refs = refs[-7 - sends :]
    natural_ref, last_ref, x_out, triple_ref = refs[:4]
    send_refs, (w_buf, x_sem, w_sem) = refs[4:-3], refs[-3:]
    slot = sent_slot(info)
    w_copy = pltpu.make_async_copy(w_ref.at[slot], w_buf, w_sem)
    w_copy.start()
    pieces = []
    for first in range(0, HALF, block):
        columns = column_span(info, other, first, block)
        copy = pltpu.make_async_copy(
            x_ref.at[:, columns, :], x_out.at[:, columns, :], x_sem.at[len(pieces)]
        )
        copy.start()
        pieces.append((copy, first, columns))
    w_copy.wait()
    w = w_buf[...]
    each = HALF // sends
    for copy, first, columns in pieces:
        copy.wait()
        send_ref = send_refs[first // each].at[pl.ds(first % each, block)]
        projected(
            x_out[:, columns, :],
            w,
            natural_ref,
            last_ref,
            (triple_ref.at[slot, pl.ds(first, block)], send_ref),
            slot,
            columns,
        )


def rest_kernel(info, x_ref, w_ref, *refs, block):
    natural_ref, mine_ref, other_ref, last_ref = refs[-4:]
    for slot in (2 - sent_slot(info), 1):
        w = w_ref[slot]
        for other, triple_ref in ((False, mine_ref), (True, other_ref)):
            for first in range(0, HALF, block):
                columns = column_span(info, other, first, block)
                projected(
                    x_ref[:, columns, :],
                    w,
                    natural_ref,
                    last_ref,
                    (triple_ref.at[slot, pl.ds(first, block)],),
                    slot,
                    columns,
                )


def project_sent(info, x, w, kept, other, sends, block=64):
    width = w.shape[2]
    shared = [(3, STRIP, COLS, width), (2, COLS, width), x.shape]
    own = [(3, HALF, STRIP, width)] + [(HALF // sends, STRIP, width)] * sends
    return call(
        functools.partial(sent_kernel, other=other, sends=sends, block=block),
        info,
        [x, w] + list(kept),
        [jax.ShapeDtypeStruct(shape, BF16) for shape in shared + own],
        [
            pltpu.VMEM(w.shape[1:], BF16),
            pltpu.SemaphoreType.DMA((HALF // block,)),
            pltpu.SemaphoreType.DMA,
        ],
        in_specs=[ANYWHERE] * 2 + [ON_CHIP] * len(kept),
        aliases={3 + n: n for n in range(len(kept))},
        name="project_sent",
    )


def project_rest(info, x, w, kept, block=64):
    return call(
        functools.partial(rest_kernel, block=block),
        info,
        [x, w] + list(kept),
        [jax.ShapeDtypeStruct(array.shape, BF16) for array in kept],
        aliases={3 + n: n for n in range(len(kept))},
        name="project_rest",
    )


def heads_of(shape, axis):
    return iota(shape, axis) // HEAD_DIM


def head_rows(rows_per_head, width):
    shape = (rows_per_head * (width // HEAD_DIM), width)
    own = iota(shape, 0) // rows_per_head == iota(shape, 1) // HEAD_DIM
    return jnp.where(own, 1.0 / math.sqrt(HEAD_DIM), 0.0).astype(BF16)


def row_kernel(info, *refs, width, top, rows):
    before_k_ref, before_v_ref, q_ref, k_ref, v_ref, out_ref, prev_k, prev_v = refs
    step = pl.program_id(0)
    heads = width // HEAD_DIM

    @pl.when(step == 0)
    def _():
        prev_k[...] = before_k_ref[0] if top else before_k_ref[0, 0]
        prev_v[...] = before_v_ref[0] if top else before_v_ref[0, 0]

    own = iota((COLS, COLS), 1) <= iota((COLS, COLS), 0)
    lane_head = heads_of((COLS, width), 1)
    scale = 1.0 / math.sqrt(HEAD_DIM)
    spread = [jnp.where(lane_head == h, scale, 0.0).astype(BF16) for h in range(heads)]
    earlier_k, earlier_v = prev_k[...], prev_v[...]
    for r in range(rows):
        q, k, v = q_ref[0, r], k_ref[0, r], v_ref[0, r]
        result = None
        for h in range(heads):
            masked = q * spread[h]
            scores_prev = dot_t(masked, earlier_k)
            if top and r == 0:
                first = (step == 0) & (info[2] == 0)
                scores_prev = scores_prev + jnp.where(first, NEG_BIG, 0.0)
            scores = jnp.where(own, dot_t(masked, k), scores_prev)
            terms = jnp.exp(scores - jnp.max(scores, axis=1, keepdims=True))
            inverse = 1.0 / jnp.sum(terms, axis=1, keepdims=True)
            context = dot(jnp.where(own, terms, 0.0).astype(BF16), v)
            context = context + dot(jnp.where(own, 0.0, terms).astype(BF16), earlier_v)
            context = context * inverse
            result = context if h == 0 else jnp.where(lane_head == h, context, result)
        out_ref[r] = result
        earlier_k, earlier_v = k, v
    prev_k[...] = earlier_k
    prev_v[...] = earlier_v


def row_part(info, halo, natural, first_row, row_count, rows=4):
    width = natural.shape[3]
    top = first_row == 0
    block = (1, rows, COLS, width)

    def spec(slot):
        return pl.BlockSpec(block, lambda r, info: (slot, first_row // rows + r, 0, 0))

    def before_spec(slot):
        if top:
            return pl.BlockSpec((1, COLS, width), lambda r, info: (slot - 1, 0, 0))
        return pl.BlockSpec((1, 1, COLS, width), lambda r, info: (slot, first_row - 1, 0, 0))

    return call(
        functools.partial(row_kernel, width=width, top=top, rows=rows),
        info,
        [halo if top else natural] * 2 + [natural] * 3,
        jax.ShapeDtypeStruct((row_count, COLS, width), F32),
        [pltpu.VMEM((COLS, width), BF16)] * 2,
        grid=(row_count // rows,),
        in_specs=[before_spec(1), before_spec(2)] + [spec(slot) for slot in range(3)],
        out_specs=pl.BlockSpec((rows, COLS, width), lambda r, info: (r, 0, 0)),
        flops=LONG,
        name="row_attention",
    )


def column_of(mine, other, j):
    return jnp.concatenate([mine[j], other[j]], 0)


def scores_of(keys, queries, spread, heads):
    return dot_t(keys, jnp.concatenate([queries] * heads, 0) * spread)


def later_key(core, heads):
    shape = (BOTH, heads * BOTH)
    key_row = (iota(shape, 0) + STRIP * core) & (BOTH - 1)
    query_row = (iota(shape, 1) + STRIP * core) & (BOTH - 1)
    return key_row > query_row


def by_pack(first, count, body):
    def run(g, carry):
        body(g, pl.ds(first + g * PACK, PACK))
        return carry

    lax.fori_loop(0, count // PACK, run, 0, unroll=8)


def maxima_kernel(info, mine_ref, other_ref, out_ref, *, heads):
    hidden = later_key(info[0], heads)
    spread = head_rows(BOTH, heads * HEAD_DIM)

    def body(g, part):
        qm, qo = mine_ref[0, part], other_ref[0, part]
        km, ko = mine_ref[1, part], other_ref[1, part]
        tops = []
        for j in range(PACK):
            scores = scores_of(column_of(km, ko, j), column_of(qm, qo, j), spread, heads)
            tops.append(jnp.max(jnp.where(hidden, NEG_BIG, scores), axis=0, keepdims=True))
        out_ref[part] = jnp.concatenate(tops, 0)

    @pl.when(info[1] == 1)
    def _():
        by_pack(0, mine_ref.shape[1], body)


def maxima(info, mine, other):
    heads = mine.shape[-1] // HEAD_DIM
    return call(
        functools.partial(maxima_kernel, heads=heads),
        info,
        [mine, other],
        jax.ShapeDtypeStruct((mine.shape[1], heads * BOTH), F32),
        name="maxima",
    )


def weights_kernel(
    info, qm_ref, qo_ref, mine_ref, other_ref, top_ref, w_ref, stats, *, heads, first, cols, base
):
    spread = head_rows(BOTH, heads * HEAD_DIM)

    def body(g, part):
        qm, qo = qm_ref[part], qo_ref[pl.ds(first - base + g * PACK, PACK)]
        km, ko = mine_ref[1, part], other_ref[1, part]
        below = top_ref[part]
        tops, totals, turned = [], [], []
        for j in range(PACK):
            scores = scores_of(column_of(km, ko, j), column_of(qm, qo, j), spread, heads)
            top = jnp.maximum(jnp.max(scores, axis=0, keepdims=True), below[j : j + 1])
            terms = jnp.exp(scores - top)
            tops.append(top)
            totals.append(jnp.sum(terms, axis=0, keepdims=True))
            turned.append(terms)
        w_ref[pl.ds(g * heads * BOTH, heads * BOTH)] = jnp.concatenate(turned, 0).T.astype(BF16)
        stats[0, pl.ds(g * PACK, PACK)] = jnp.concatenate(tops, 0)
        stats[1, pl.ds(g * PACK, PACK)] = jnp.concatenate(totals, 0)

    @pl.when(info[1] == 0)
    def _():
        by_pack(first, cols, body)
        rest = stats[...].reshape(2 * cols, heads * BOTH)
        at = cols // PACK * heads * BOTH
        for n in range(SLICES):
            part = rest.astype(BF16)
            w_ref[at + n * 2 * cols : at + (n + 1) * 2 * cols] = part
            rest = rest - part.astype(F32)


def cross_weights(info, recv_mine, recv_other, mine, other, top, first, cols, base):
    heads = mine.shape[-1] // HEAD_DIM
    rows = heads * BOTH
    return call(
        functools.partial(weights_kernel, heads=heads, first=first, cols=cols, base=base),
        info,
        [recv_mine, recv_other, mine, other, top],
        jax.ShapeDtypeStruct((cols // PACK * rows + SLICES * 2 * cols, PACK * BOTH), BF16),
        [pltpu.VMEM((2, cols, rows), F32)],
        name="cross_weights",
    )


def column_kernel(
    info, mine_ref, other_ref, vm_ref, vo_ref, w_ref, om_ref, oo_ref, stats, *, heads, first, cols, base
):
    hidden = later_key(info[0], heads)
    width = heads * HEAD_DIM
    rows = heads * BOTH
    spread = head_rows(BOTH, width)
    lower = info[1] == 1
    pair = 2 * BOTH
    keys = PACK * BOTH
    key_column = (iota((1, 2 * keys), 1) & (keys - 1)) // BOTH
    picks = [jnp.where(key_column == j, 1.0, 0.0).astype(BF16) for j in range(PACK)]
    left_head = iota((BOTH, 2 * HEAD_DIM), 1) < HEAD_DIM
    at = cols // PACK * rows
    whole = w_ref[at : at + 2 * cols].astype(F32)
    for n in range(1, SLICES):
        whole = whole + w_ref[at + n * 2 * cols : at + (n + 1) * 2 * cols].astype(F32)
    stats[...] = whole.reshape(stats.shape)

    def body(g, part):
        local = pl.ds(g * PACK, PACK)
        qm, qo = mine_ref[0, part], other_ref[0, part]
        km, ko = mine_ref[1, part], other_ref[1, part]
        above, far_totals = stats[0, local], stats[1, local]
        totals, turned = [], []
        for j in range(PACK):
            scores = scores_of(column_of(km, ko, j), column_of(qm, qo, j), spread, heads)
            scores = jnp.where(hidden, NEG_BIG, scores)
            top = jnp.max(scores, axis=0, keepdims=True)
            top = jnp.where(lower, above[j : j + 1], top)
            terms = jnp.exp(scores - top)
            totals.append(jnp.sum(terms, axis=0, keepdims=True))
            turned.append(terms)
        inverse = 1.0 / (jnp.concatenate(totals, 0) + far_totals)
        inverse = jnp.concatenate([inverse, inverse], 0).T
        near = jnp.concatenate(turned, 0).T.astype(BF16)
        weights = jnp.concatenate([near, w_ref[pl.ds(g * rows, rows)]], 1)
        near_v = [column_of(mine_ref[2, part], other_ref[2, part], j) for j in range(PACK)]
        vm, vo = vm_ref[part], vo_ref[pl.ds(first - base + g * PACK, PACK)]
        far_v = [column_of(vm, vo, j) for j in range(PACK)]
        values = jnp.concatenate(near_v + far_v, 0)
        left = jnp.concatenate([weights * picks[j] for j in range(PACK)], 0)
        context = dot(left, values)
        for j in range(PACK):
            outs = []
            for t in range(heads // 2):
                lanes = slice(t * 2 * HEAD_DIM, (t + 1) * 2 * HEAD_DIM)
                at = j * rows + t * pair
                head = t * pair
                out = jnp.where(
                    left_head,
                    context[at : at + BOTH, lanes],
                    context[at + BOTH : at + 2 * BOTH, lanes],
                )
                factor = jnp.where(
                    left_head,
                    inverse[head : head + BOTH, j : j + 1],
                    inverse[head + BOTH : head + 2 * BOTH, j : j + 1],
                )
                outs.append((out * factor).astype(BF16))
            out = jnp.concatenate(outs, 1)
            om_ref[g * PACK + j] = out[:STRIP]
            oo_ref[g * PACK + j] = out[STRIP:]

    by_pack(first, cols, body)


def column_part(info, mine, other, recv_mine, recv_other, weights, first, cols, base, flops):
    width = mine.shape[-1]
    heads = width // HEAD_DIM
    shape = jax.ShapeDtypeStruct((cols, STRIP, width), BF16)
    return call(
        functools.partial(column_kernel, heads=heads, first=first, cols=cols, base=base),
        info,
        [mine, other, recv_mine, recv_other, weights],
        [shape, shape],
        [pltpu.VMEM((2, cols, heads * BOTH), F32)],
        flops=flops,
        name="column_attention",
    )


def mix_kernel(info, *refs, first, cols, parts):
    row_refs, near_ref, far_ref = refs[:parts], refs[parts], refs[parts + 1]
    out_ref, out_buf, out_sem = refs[-3:]
    copies = []
    for o, ref in enumerate((near_ref, far_ref)):
        span = column_span(info, o == 1, first, cols)
        column = jnp.swapaxes(ref[...], 0, 1).astype(F32)
        at = 0
        for row_ref in row_refs:
            rows = slice(at, at + row_ref.shape[0])
            out_buf[o, rows] = (0.5 * (row_ref[:, span, :] + column[rows])).astype(BF16)
            at += row_ref.shape[0]
        copy = pltpu.make_async_copy(out_buf.at[o], out_ref.at[:, span, :], out_sem.at[o])
        copy.start()
        copies.append(copy)
    for copy in copies:
        copy.wait()


def mix(info, row_context, near, far, done, first):
    cols, _, width = near.shape
    parts = len(row_context)
    operands = list(row_context) + [near, far]
    in_specs = [ON_CHIP] * len(operands)
    aliases = {}
    if done is not None:
        operands.append(done)
        in_specs.append(ANYWHERE)
        aliases = {len(operands): 0}
    return call(
        functools.partial(mix_kernel, first=first, cols=cols, parts=parts),
        info,
        operands,
        jax.ShapeDtypeStruct((STRIP, COLS, width), BF16),
        [pltpu.VMEM((2, STRIP, cols, width), BF16), pltpu.SemaphoreType.DMA((2,))],
        in_specs=in_specs,
        out_specs=ANYWHERE,
        aliases=aliases,
        name="mix",
    )


CORE_SWAP = [(0, 1), (1, 0), (2, 3), (3, 2)]
SAME_CORE = [(0, 2), (1, 3), (2, 0), (3, 1)]
OTHER_CORE = [(0, 3), (1, 2), (2, 1), (3, 0)]
DOWN_SAME = [(0, 2), (1, 3)]
UP_SAME = [(2, 0), (3, 1)]
NEXT_STRIP = [(0, 1), (1, 2), (2, 3)]


def send(block, route):
    return pltpu.with_memory_space_constraint(lax.ppermute(block, "seq", route), pltpu.VMEM)


def in_hbm(array):
    return pltpu.with_memory_space_constraint(array, pltpu.HBM)


def after(value, *earlier):
    return lax.optimization_barrier((value,) + earlier)[0]


def two_chips(patches, w_qkv):
    width = w_qkv.shape[2]
    chunks = ((0, 64), (64, 32), (96, 32))
    seq = lax.axis_index("seq")
    info = jnp.stack([seq % 2, seq // 2, seq]).astype(jnp.int32)
    x = patches.reshape(STRIP, COLS, D)
    w = jnp.transpose(w_qkv, (1, 0, 2))

    x, from_hbm = in_hbm(x), in_hbm(w)
    *shared, mine, sent = project_sent(info, x, from_hbm, (), False, 1)
    recv_mine = send(sent, SAME_CORE)
    *shared, other, sent, sent_later = project_sent(info, x, from_hbm, shared, True, 2)
    natural, last, x = shared
    natural, mine, other, last = project_rest(info, x, w, (natural, mine, other, last))
    other = send(other, CORE_SWAP)
    halo = send(last, NEXT_STRIP)
    recv_others = [send(after(sent, last), OTHER_CORE)]
    info = after(info, recv_mine, halo)
    rows_low = row_part(info, None, natural, 12, 4)
    info = after(info, rows_low)
    top = maxima(info, mine, other)
    below = send(top, UP_SAME)
    recv_others.append(send(after(sent_later, top), OTHER_CORE))
    info = after(info, top)
    far = []
    for n, (at, cols) in enumerate(chunks):
        part = at // SPLIT
        weights = cross_weights(
            info, recv_mine, recv_others[part], mine, other, below, at, cols, part * SPLIT
        )
        info = after(info, weights)
        far.append(send(weights, DOWN_SAME))
        if n == 0:
            rows_top = row_part(info, halo, natural, 0, 12)
            info = after(info, rows_top)
    row_context = (rows_top, rows_low)
    pending = []
    out = None
    for n, ((at, cols), weights) in enumerate(zip(chunks, far)):
        part = at // SPLIT
        near, remote = column_part(
            info,
            mine,
            other,
            recv_mine,
            recv_others[part],
            weights,
            at,
            cols,
            part * SPLIT,
            LONG if n > 0 else 1,
        )
        info = after(info, near)
        pending.append((near, send(remote, CORE_SWAP), at))
        if n > 0:
            near, remote, at = pending.pop(0)
            out = mix(info, row_context, near, remote, out, at)
            info = after(info, out)
    near, remote, at = pending.pop(0)
    out = mix(info, row_context, near, remote, out, at)
    return out.reshape(STRIP * COLS, width)


def local(patches, w_qkv):
    shape_fits = patches.shape[0] == STRIP * COLS and w_qkv.shape[2] == 4 * HEAD_DIM
    if lax.axis_size("seq") == 4 and shape_fits:
        return two_chips(patches, w_qkv)
    return general(patches, w_qkv)


def solution(mesh):
    placed = (P(("groups", "seq"), None), P(None, None, "head"))
    return jax.shard_map(
        local, mesh=mesh, in_specs=placed, out_specs=P(("groups", "seq"), "head"), check_vma=False
    )
```

```python
import functools
import math

import jax
import jax.numpy as jnp
from jax import lax
from jax.experimental import pallas as pl
from jax.experimental.pallas import tpu as pltpu
from jax.sharding import PartitionSpec as P

D = 1024
HEAD_DIM = 64
COLS = 256
NEG_BIG = -1e30

STRIP = 16
BOTH = 2 * STRIP
PACK = 4

F32 = jnp.float32
BF16 = jnp.bfloat16


def shifted(block, axis, distance):
    devices = range(lax.axis_size(axis))
    route = [(i - distance, i) for i in devices if i - distance in devices]
    return lax.ppermute(block, axis, route)


def row_attention(queries, key_rows, value_rows, prev_keys, prev_values, first_row):
    row_count = queries.shape[1]
    scale = 1.0 / math.sqrt(HEAD_DIM)
    earlier_keys = jnp.concatenate([prev_keys[:, None], key_rows[:, :-1]], 1)
    earlier_values = jnp.concatenate([prev_values[:, None], value_rows[:, :-1]], 1)
    score_prev = (
        jnp.einsum("hrce,hrje->hrcj", queries, earlier_keys, preferred_element_type=jnp.float32)
        * scale
    )
    score_own = (
        jnp.einsum("hrce,hrje->hrcj", queries, key_rows, preferred_element_type=jnp.float32) * scale
    )
    column = lax.broadcasted_iota(jnp.int32, (1, 1, COLS, COLS), 2)
    slot = lax.broadcasted_iota(jnp.int32, (1, 1, COLS, COLS), 3)
    row_index = lax.broadcasted_iota(jnp.int32, (1, row_count, 1, 1), 1) + first_row
    allowed_prev = (slot > column) & (row_index > 0)
    allowed_own = slot <= column
    score_prev = jnp.where(allowed_prev, score_prev, NEG_BIG)
    score_own = jnp.where(allowed_own, score_own, NEG_BIG)
    highest = jnp.maximum(
        jnp.max(score_prev, axis=-1, keepdims=True), jnp.max(score_own, axis=-1, keepdims=True)
    )
    terms_prev = jnp.where(allowed_prev, jnp.exp(score_prev - highest), 0.0)
    terms_own = jnp.where(allowed_own, jnp.exp(score_own - highest), 0.0)
    totals = jnp.sum(terms_prev, axis=-1, keepdims=True) + jnp.sum(
        terms_own, axis=-1, keepdims=True
    )
    context = jnp.einsum(
        "hrcj,hrje->hrce",
        terms_prev.astype(jnp.bfloat16),
        earlier_values,
        preferred_element_type=jnp.float32,
    )
    context = context + jnp.einsum(
        "hrcj,hrje->hrce",
        terms_own.astype(jnp.bfloat16),
        value_rows,
        preferred_element_type=jnp.float32,
    )
    return context / totals


def column_attention(queries, key_rows, value_rows):
    row_count = queries.shape[1]
    scores = jnp.einsum(
        "hrce,hsce->hcrs", queries, key_rows, preferred_element_type=jnp.float32
    ) * (1.0 / math.sqrt(HEAD_DIM))
    later = lax.broadcasted_iota(jnp.int32, (1, 1, row_count, row_count), 2)
    earlier = lax.broadcasted_iota(jnp.int32, (1, 1, row_count, row_count), 3)
    allowed = earlier <= later
    scores = jnp.where(allowed, scores, NEG_BIG)
    highest = jnp.max(scores, axis=-1, keepdims=True)
    terms = jnp.where(allowed, jnp.exp(scores - highest), 0.0)
    totals = jnp.sum(terms, axis=-1, keepdims=True)
    context = jnp.einsum(
        "hcrs,hsce->hcre",
        terms.astype(jnp.bfloat16),
        value_rows,
        preferred_element_type=jnp.float32,
    )
    return jnp.transpose((context / totals).astype(jnp.bfloat16), (0, 2, 1, 3))


def general(patches, w_qkv):
    local_width = w_qkv.shape[2]
    head_count = local_width // HEAD_DIM
    row_count = patches.shape[0] // COLS
    weights_heads = w_qkv.reshape(D, 3, head_count, HEAD_DIM)
    projected = jnp.einsum(
        "td,dkhe->khte", patches, weights_heads, preferred_element_type=jnp.float32
    ).astype(jnp.bfloat16)
    prev_inputs = shifted(patches[-COLS:], "seq", 1)
    prev_pair = jnp.einsum(
        "td,dkhe->khte", prev_inputs, weights_heads[:, 1:], preferred_element_type=jnp.float32
    ).astype(jnp.bfloat16)
    first_row = lax.axis_index("seq") * row_count
    stacked = projected.reshape(3, head_count, row_count, COLS, HEAD_DIM)
    row_context = row_attention(
        stacked[0], stacked[1], stacked[2], prev_pair[0], prev_pair[1], first_row
    )
    column_pack = lax.all_to_all(stacked, "seq", split_axis=3, concat_axis=2, tiled=True)
    column_context = column_attention(column_pack[0], column_pack[1], column_pack[2])
    returned = lax.all_to_all(column_context, "seq", split_axis=1, concat_axis=2, tiled=True)
    mixed = (0.5 * (row_context + returned.astype(jnp.float32))).astype(jnp.bfloat16)
    return jnp.transpose(mixed, (1, 2, 0, 3)).reshape(row_count * COLS, local_width)


def iota(shape, axis):
    return lax.broadcasted_iota(jnp.int32, shape, axis)


def dot(left, right):
    return jnp.dot(left, right, preferred_element_type=F32)


def dot_t(left, right):
    return lax.dot_general(left, right, (((1,), (1,)), ((), ())), preferred_element_type=F32)


SLICES = 3
HALF = COLS // 2
LONG = 4 * 10**10
SPLIT = HALF // 2
ANYWHERE = pl.BlockSpec(memory_space=pl.ANY)
ON_CHIP = pl.BlockSpec(memory_space=pltpu.VMEM)


def call(kernel, info, operands, out_shape, scratch=(), **more):
    options = dict(
        in_specs=[ON_CHIP] * len(operands),
        out_specs=jax.tree.map(lambda _: ON_CHIP, out_shape),
    )
    aliases = more.pop("aliases", {})
    name = more.pop("name")
    flops = more.pop("flops", 1)
    options.update(more)
    return pl.pallas_call(
        kernel,
        out_shape=out_shape,
        grid_spec=pltpu.PrefetchScalarGridSpec(
            num_scalar_prefetch=1,
            grid=options.pop("grid", ()),
            scratch_shapes=list(scratch),
            **options,
        ),
        input_output_aliases=aliases,
        compiler_params=pltpu.CompilerParams(vmem_limit_bytes=20 << 20),
        cost_estimate=pl.CostEstimate(flops=flops, bytes_accessed=1, transcendentals=0),
        name=name,
    )(info, *operands)


def column_span(info, other, first, cols):
    half = 1 - info[0] if other else info[0]
    return pl.ds(pl.multiple_of(half * HALF + first, 16), cols)


def sent_slot(info):
    return jnp.where(info[1] == 0, 2, 0)


def projected(x, w, natural_ref, last_ref, turned_refs, slot, columns):
    _, block, depth = x.shape
    part = STRIP // 2
    parts = [
        dot(x[r : r + part].reshape(part * block, depth), w).astype(BF16) for r in (0, part)
    ]
    value = jnp.concatenate(parts, 0).reshape(STRIP, block, w.shape[1])
    natural_ref[slot, :, columns, :] = value

    @pl.when(slot > 0)
    def _():
        last_ref[slot - 1, columns, :] = value[STRIP - 1]

    turned = jnp.swapaxes(value, 0, 1)
    for ref in turned_refs:
        ref[...] = turned


def sent_kernel(info, x_ref, w_ref, *refs, other, start, cols, sends, block):
    refs = refs[-7 - sends :]
    natural_ref, last_ref, x_out, triple_ref = refs[:4]
    send_refs, (w_buf, x_sem, w_sem) = refs[4:-3], refs[-3:]
    slot = sent_slot(info)
    w_copy = pltpu.make_async_copy(w_ref.at[slot], w_buf, w_sem)
    w_copy.start()
    pieces = []
    for first in range(start, start + cols, block):
        columns = column_span(info, other, first, block)
        copy = pltpu.make_async_copy(
            x_ref.at[:, columns, :], x_out.at[:, columns, :], x_sem.at[len(pieces)]
        )
        copy.start()
        pieces.append((copy, first, columns))
    w_copy.wait()
    w = w_buf[...]
    each = cols // sends
    for copy, first, columns in pieces:
        copy.wait()
        send_ref = send_refs[(first - start) // each].at[pl.ds((first - start) % each, block)]
        projected(
            x_out[:, columns, :],
            w,
            natural_ref,
            last_ref,
            (triple_ref.at[slot, pl.ds(first, block)], send_ref),
            slot,
            columns,
        )


def rest_kernel(info, x_ref, w_ref, *refs, block):
    natural_ref, mine_ref, other_ref, last_ref = refs[-4:]
    for slot in (2 - sent_slot(info), 1):
        w = w_ref[slot]
        for other, triple_ref in ((False, mine_ref), (True, other_ref)):
            for first in range(0, HALF, block):
                columns = column_span(info, other, first, block)
                projected(
                    x_ref[:, columns, :],
                    w,
                    natural_ref,
                    last_ref,
                    (triple_ref.at[slot, pl.ds(first, block)],),
                    slot,
                    columns,
                )


def project_sent(info, x, w, kept, other, start, cols, sends, block=64):
    width = w.shape[2]
    shared = [(3, STRIP, COLS, width), (2, COLS, width), x.shape]
    own = [(3, HALF, STRIP, width)] + [(cols // sends, STRIP, width)] * sends
    return call(
        functools.partial(
            sent_kernel, other=other, start=start, cols=cols, sends=sends, block=block
        ),
        info,
        [x, w] + list(kept),
        [jax.ShapeDtypeStruct(shape, BF16) for shape in shared + own],
        [
            pltpu.VMEM(w.shape[1:], BF16),
            pltpu.SemaphoreType.DMA((cols // block,)),
            pltpu.SemaphoreType.DMA,
        ],
        in_specs=[ANYWHERE] * 2 + [ON_CHIP] * len(kept),
        aliases={3 + n: n for n in range(len(kept))},
        name="project_sent",
    )


def project_rest(info, x, w, kept, block=64):
    return call(
        functools.partial(rest_kernel, block=block),
        info,
        [x, w] + list(kept),
        [jax.ShapeDtypeStruct(array.shape, BF16) for array in kept],
        aliases={3 + n: n for n in range(len(kept))},
        name="project_rest",
    )


def heads_of(shape, axis):
    return iota(shape, axis) // HEAD_DIM


def head_rows(rows_per_head, width):
    shape = (rows_per_head * (width // HEAD_DIM), width)
    own = iota(shape, 0) // rows_per_head == iota(shape, 1) // HEAD_DIM
    return jnp.where(own, 1.0 / math.sqrt(HEAD_DIM), 0.0).astype(BF16)


def row_kernel(info, *refs, width, top, rows):
    before_k_ref, before_v_ref, q_ref, k_ref, v_ref, out_ref, prev_k, prev_v = refs
    step = pl.program_id(0)
    heads = width // HEAD_DIM

    @pl.when(step == 0)
    def _():
        prev_k[...] = before_k_ref[0] if top else before_k_ref[0, 0]
        prev_v[...] = before_v_ref[0] if top else before_v_ref[0, 0]

    own = iota((COLS, COLS), 1) <= iota((COLS, COLS), 0)
    lane_head = heads_of((COLS, width), 1)
    scale = 1.0 / math.sqrt(HEAD_DIM)
    spread = [jnp.where(lane_head == h, scale, 0.0).astype(BF16) for h in range(heads)]
    earlier_k, earlier_v = prev_k[...], prev_v[...]
    for r in range(rows):
        q, k, v = q_ref[0, r], k_ref[0, r], v_ref[0, r]
        result = None
        for h in range(heads):
            masked = q * spread[h]
            scores_prev = dot_t(masked, earlier_k)
            if top and r == 0:
                first = (step == 0) & (info[2] == 0)
                scores_prev = scores_prev + jnp.where(first, NEG_BIG, 0.0)
            scores = jnp.where(own, dot_t(masked, k), scores_prev)
            terms = jnp.exp(scores - jnp.max(scores, axis=1, keepdims=True))
            inverse = 1.0 / jnp.sum(terms, axis=1, keepdims=True)
            context = dot(jnp.where(own, terms, 0.0).astype(BF16), v)
            context = context + dot(jnp.where(own, 0.0, terms).astype(BF16), earlier_v)
            context = context * inverse
            result = context if h == 0 else jnp.where(lane_head == h, context, result)
        out_ref[r] = result
        earlier_k, earlier_v = k, v
    prev_k[...] = earlier_k
    prev_v[...] = earlier_v


def row_part(info, halo, natural, first_row, row_count, rows=4):
    width = natural.shape[3]
    top = first_row == 0
    block = (1, rows, COLS, width)

    def spec(slot):
        return pl.BlockSpec(block, lambda r, info: (slot, first_row // rows + r, 0, 0))

    def before_spec(slot):
        if top:
            return pl.BlockSpec((1, COLS, width), lambda r, info: (slot - 1, 0, 0))
        return pl.BlockSpec((1, 1, COLS, width), lambda r, info: (slot, first_row - 1, 0, 0))

    return call(
        functools.partial(row_kernel, width=width, top=top, rows=rows),
        info,
        [halo if top else natural] * 2 + [natural] * 3,
        jax.ShapeDtypeStruct((row_count, COLS, width), F32),
        [pltpu.VMEM((COLS, width), BF16)] * 2,
        grid=(row_count // rows,),
        in_specs=[before_spec(1), before_spec(2)] + [spec(slot) for slot in range(3)],
        out_specs=pl.BlockSpec((rows, COLS, width), lambda r, info: (r, 0, 0)),
        flops=LONG,
        name="row_attention",
    )


def column_of(mine, other, j):
    return jnp.concatenate([mine[j], other[j]], 0)


def scores_of(keys, queries, spread, heads):
    return dot_t(keys, jnp.concatenate([queries] * heads, 0) * spread)


def later_key(core, heads):
    shape = (BOTH, heads * BOTH)
    key_row = (iota(shape, 0) + STRIP * core) & (BOTH - 1)
    query_row = (iota(shape, 1) + STRIP * core) & (BOTH - 1)
    return key_row > query_row


def by_pack(first, count, body):
    def run(g, carry):
        body(g, pl.ds(first + g * PACK, PACK))
        return carry

    lax.fori_loop(0, count // PACK, run, 0, unroll=8)


def maxima_kernel(info, mine_ref, other_ref, out_ref, *, heads):
    hidden = later_key(info[0], heads)
    spread = head_rows(BOTH, heads * HEAD_DIM)

    def body(g, part):
        qm, qo = mine_ref[0, part], other_ref[0, part]
        km, ko = mine_ref[1, part], other_ref[1, part]
        tops = []
        for j in range(PACK):
            scores = scores_of(column_of(km, ko, j), column_of(qm, qo, j), spread, heads)
            tops.append(jnp.max(jnp.where(hidden, NEG_BIG, scores), axis=0, keepdims=True))
        out_ref[part] = jnp.concatenate(tops, 0)

    @pl.when(info[1] == 1)
    def _():
        by_pack(0, mine_ref.shape[1], body)


def maxima(info, mine, other):
    heads = mine.shape[-1] // HEAD_DIM
    return call(
        functools.partial(maxima_kernel, heads=heads),
        info,
        [mine, other],
        jax.ShapeDtypeStruct((mine.shape[1], heads * BOTH), F32),
        name="maxima",
    )


def weights_kernel(
    info, qm_ref, qo_ref, mine_ref, other_ref, top_ref, w_ref, stats, *, heads, first, cols, base
):
    spread = head_rows(BOTH, heads * HEAD_DIM)

    def body(g, part):
        near = pl.ds(first - base + g * PACK, PACK)
        qm, qo = qm_ref[near], qo_ref[near]
        km, ko = mine_ref[1, part], other_ref[1, part]
        below = top_ref[part]
        tops, totals, turned = [], [], []
        for j in range(PACK):
            scores = scores_of(column_of(km, ko, j), column_of(qm, qo, j), spread, heads)
            top = jnp.maximum(jnp.max(scores, axis=0, keepdims=True), below[j : j + 1])
            terms = jnp.exp(scores - top)
            tops.append(top)
            totals.append(jnp.sum(terms, axis=0, keepdims=True))
            turned.append(terms)
        w_ref[pl.ds(g * heads * BOTH, heads * BOTH)] = jnp.concatenate(turned, 0).T.astype(BF16)
        stats[0, pl.ds(g * PACK, PACK)] = jnp.concatenate(tops, 0)
        stats[1, pl.ds(g * PACK, PACK)] = jnp.concatenate(totals, 0)

    @pl.when(info[1] == 0)
    def _():
        by_pack(first, cols, body)
        rest = stats[...].reshape(2 * cols, heads * BOTH)
        at = cols // PACK * heads * BOTH
        for n in range(SLICES):
            part = rest.astype(BF16)
            w_ref[at + n * 2 * cols : at + (n + 1) * 2 * cols] = part
            rest = rest - part.astype(F32)


def cross_weights(info, recv_mine, recv_other, mine, other, top, first, cols, base):
    heads = mine.shape[-1] // HEAD_DIM
    rows = heads * BOTH
    return call(
        functools.partial(weights_kernel, heads=heads, first=first, cols=cols, base=base),
        info,
        [recv_mine, recv_other, mine, other, top],
        jax.ShapeDtypeStruct((cols // PACK * rows + SLICES * 2 * cols, PACK * BOTH), BF16),
        [pltpu.VMEM((2, cols, rows), F32)],
        name="cross_weights",
    )


def column_kernel(
    info, mine_ref, other_ref, vm_ref, vo_ref, w_ref, om_ref, oo_ref, stats, *, heads, first, cols, base
):
    hidden = later_key(info[0], heads)
    width = heads * HEAD_DIM
    rows = heads * BOTH
    spread = head_rows(BOTH, width)
    lower = info[1] == 1
    pair = 2 * BOTH
    keys = PACK * BOTH
    key_column = (iota((1, 2 * keys), 1) & (keys - 1)) // BOTH
    picks = [jnp.where(key_column == j, 1.0, 0.0).astype(BF16) for j in range(PACK)]
    left_head = iota((BOTH, 2 * HEAD_DIM), 1) < HEAD_DIM
    at = cols // PACK * rows
    whole = w_ref[at : at + 2 * cols].astype(F32)
    for n in range(1, SLICES):
        whole = whole + w_ref[at + n * 2 * cols : at + (n + 1) * 2 * cols].astype(F32)
    stats[...] = whole.reshape(stats.shape)

    def body(g, part):
        local = pl.ds(g * PACK, PACK)
        qm, qo = mine_ref[0, part], other_ref[0, part]
        km, ko = mine_ref[1, part], other_ref[1, part]
        above, far_totals = stats[0, local], stats[1, local]
        totals, turned = [], []
        for j in range(PACK):
            scores = scores_of(column_of(km, ko, j), column_of(qm, qo, j), spread, heads)
            scores = jnp.where(hidden, NEG_BIG, scores)
            top = jnp.max(scores, axis=0, keepdims=True)
            top = jnp.where(lower, above[j : j + 1], top)
            terms = jnp.exp(scores - top)
            totals.append(jnp.sum(terms, axis=0, keepdims=True))
            turned.append(terms)
        inverse = 1.0 / (jnp.concatenate(totals, 0) + far_totals)
        inverse = jnp.concatenate([inverse, inverse], 0).T
        near = jnp.concatenate(turned, 0).T.astype(BF16)
        weights = jnp.concatenate([near, w_ref[pl.ds(g * rows, rows)]], 1)
        near_v = [column_of(mine_ref[2, part], other_ref[2, part], j) for j in range(PACK)]
        sent = pl.ds(first - base + g * PACK, PACK)
        vm, vo = vm_ref[sent], vo_ref[sent]
        far_v = [column_of(vm, vo, j) for j in range(PACK)]
        values = jnp.concatenate(near_v + far_v, 0)
        left = jnp.concatenate([weights * picks[j] for j in range(PACK)], 0)
        context = dot(left, values)
        for j in range(PACK):
            outs = []
            for t in range(heads // 2):
                lanes = slice(t * 2 * HEAD_DIM, (t + 1) * 2 * HEAD_DIM)
                at = j * rows + t * pair
                head = t * pair
                out = jnp.where(
                    left_head,
                    context[at : at + BOTH, lanes],
                    context[at + BOTH : at + 2 * BOTH, lanes],
                )
                factor = jnp.where(
                    left_head,
                    inverse[head : head + BOTH, j : j + 1],
                    inverse[head + BOTH : head + 2 * BOTH, j : j + 1],
                )
                outs.append((out * factor).astype(BF16))
            out = jnp.concatenate(outs, 1)
            om_ref[g * PACK + j] = out[:STRIP]
            oo_ref[g * PACK + j] = out[STRIP:]

    by_pack(first, cols, body)


def column_part(info, mine, other, recv_mine, recv_other, weights, first, cols, base, flops):
    width = mine.shape[-1]
    heads = width // HEAD_DIM
    shape = jax.ShapeDtypeStruct((cols, STRIP, width), BF16)
    return call(
        functools.partial(column_kernel, heads=heads, first=first, cols=cols, base=base),
        info,
        [mine, other, recv_mine, recv_other, weights],
        [shape, shape],
        [pltpu.VMEM((2, cols, heads * BOTH), F32)],
        flops=flops,
        name="column_attention",
    )


def mix_kernel(info, *refs, first, cols, parts):
    row_refs, near_ref, far_ref = refs[:parts], refs[parts], refs[parts + 1]
    out_ref, out_buf, out_sem = refs[-3:]
    copies = []
    for o, ref in enumerate((near_ref, far_ref)):
        span = column_span(info, o == 1, first, cols)
        column = jnp.swapaxes(ref[...], 0, 1).astype(F32)
        at = 0
        for row_ref in row_refs:
            rows = slice(at, at + row_ref.shape[0])
            out_buf[o, rows] = (0.5 * (row_ref[:, span, :] + column[rows])).astype(BF16)
            at += row_ref.shape[0]
        copy = pltpu.make_async_copy(out_buf.at[o], out_ref.at[:, span, :], out_sem.at[o])
        copy.start()
        copies.append(copy)
    for copy in copies:
        copy.wait()


def mix(info, row_context, near, far, done, first):
    cols, _, width = near.shape
    parts = len(row_context)
    operands = list(row_context) + [near, far]
    in_specs = [ON_CHIP] * len(operands)
    aliases = {}
    if done is not None:
        operands.append(done)
        in_specs.append(ANYWHERE)
        aliases = {len(operands): 0}
    return call(
        functools.partial(mix_kernel, first=first, cols=cols, parts=parts),
        info,
        operands,
        jax.ShapeDtypeStruct((STRIP, COLS, width), BF16),
        [pltpu.VMEM((2, STRIP, cols, width), BF16), pltpu.SemaphoreType.DMA((2,))],
        in_specs=in_specs,
        out_specs=ANYWHERE,
        aliases=aliases,
        name="mix",
    )


CORE_SWAP = [(0, 1), (1, 0), (2, 3), (3, 2)]
SAME_CORE = [(0, 2), (1, 3), (2, 0), (3, 1)]
OTHER_CORE = [(0, 3), (1, 2), (2, 1), (3, 0)]
DOWN_SAME = [(0, 2), (1, 3)]
UP_SAME = [(2, 0), (3, 1)]
NEXT_STRIP = [(0, 1), (1, 2), (2, 3)]


def send(block, route):
    return pltpu.with_memory_space_constraint(lax.ppermute(block, "seq", route), pltpu.VMEM)


def in_hbm(array):
    return pltpu.with_memory_space_constraint(array, pltpu.HBM)


def after(value, *earlier):
    return lax.optimization_barrier((value,) + earlier)[0]


def two_chips(patches, w_qkv):
    width = w_qkv.shape[2]
    chunks = ((0, 32), (32, 32), (64, 32), (96, 32))
    seq = lax.axis_index("seq")
    info = jnp.stack([seq % 2, seq // 2, seq]).astype(jnp.int32)
    x = patches.reshape(STRIP, COLS, D)
    w = jnp.transpose(w_qkv, (1, 0, 2))

    x, from_hbm = in_hbm(x), in_hbm(w)
    *shared, mine, sent = project_sent(info, x, from_hbm, (), False, 0, SPLIT, 1)
    recv_mines = [send(sent, SAME_CORE)]
    *shared, mine, sent = project_sent(
        info, x, from_hbm, shared + [mine], False, SPLIT, HALF - SPLIT, 1
    )
    recv_mines.append(send(sent, SAME_CORE))
    *shared, other, sent, sent_later = project_sent(
        info, x, from_hbm, shared, True, 0, HALF, 2
    )
    natural, last, x = shared
    natural, mine, other, last = project_rest(info, x, w, (natural, mine, other, last))
    other = send(other, CORE_SWAP)
    halo = send(last, NEXT_STRIP)
    recv_others = [send(after(sent, last), OTHER_CORE)]
    info = after(info, *recv_mines, halo)
    rows_low = row_part(info, None, natural, 12, 4)
    info = after(info, rows_low)
    top = maxima(info, mine, other)
    below = send(top, UP_SAME)
    recv_others.append(send(after(sent_later, top), OTHER_CORE))
    info = after(info, top)
    far = []
    for n, (at, cols) in enumerate(chunks):
        part = at // SPLIT
        weights = cross_weights(
            info, recv_mines[part], recv_others[part], mine, other, below, at, cols, part * SPLIT
        )
        info = after(info, weights)
        far.append(send(weights, DOWN_SAME))
        if n == 0:
            rows_top = row_part(info, halo, natural, 0, 12)
            info = after(info, rows_top)
    row_context = (rows_top, rows_low)
    pending = []
    out = None
    for n, ((at, cols), weights) in enumerate(zip(chunks, far)):
        part = at // SPLIT
        near, remote = column_part(
            info,
            mine,
            other,
            recv_mines[part],
            recv_others[part],
            weights,
            at,
            cols,
            part * SPLIT,
            LONG if n > 0 else 1,
        )
        info = after(info, near)
        pending.append((near, send(remote, CORE_SWAP), at))
        if n > 0:
            near, remote, at = pending.pop(0)
            out = mix(info, row_context, near, remote, out, at)
            info = after(info, out)
    near, remote, at = pending.pop(0)
    out = mix(info, row_context, near, remote, out, at)
    return out.reshape(STRIP * COLS, width)


def local(patches, w_qkv):
    shape_fits = patches.shape[0] == STRIP * COLS and w_qkv.shape[2] == 4 * HEAD_DIM
    if lax.axis_size("seq") == 4 and shape_fits:
        return two_chips(patches, w_qkv)
    return general(patches, w_qkv)


def solution(mesh):
    placed = (P(("groups", "seq"), None), P(None, None, "head"))
    return jax.shard_map(
        local, mesh=mesh, in_specs=placed, out_specs=P(("groups", "seq"), "head"), check_vma=False
    )
```
